32 devices in a mesh: shard: 2 (over x), ctx: 4 (over z), tp: 4 (over y, core).
Axes of the slice: x: 2, y: 2, z: 4, core: 2. Of those that a mesh axis runs over, the one named last changes fastest.
Arguments:
- x_img: bfloat16 [6, 1024, 1536], P('shard', ('ctx', 'tp')), may hold values from -6 to 6
- x_txt: bfloat16 [6, 160, 1536], P('shard', ('ctx', 'tp')), may hold values from -6 to 6
- cond: bfloat16 [6, 1536], P('shard'), may hold values from -6 to 6
- lengths: int32 [6], P('shard'), may hold values from 77 to 154, as said below
- mod_w: bfloat16 [2, 1536, 6, 1536], P(None, ('shard', 'ctx'), None, 'tp'), may hold values from -0.15625 to 0.15625
- qkv_w: bfloat16 [2, 3, 1536, 1536], P(None, None, ('shard', 'ctx'), 'tp'), may hold values from -0.15625 to 0.15625
- o_w: bfloat16 [2, 1536, 1536], P(None, 'tp', ('shard', 'ctx')), may hold values from -0.875 to 0.875
- up_w: bfloat16 [2, 1536, 6144], P(None, ('shard', 'ctx'), 'tp'), may hold values from -0.15625 to 0.15625
- down_w: bfloat16 [2, 6144, 1536], P(None, 'tp', ('shard', 'ctx')), may hold values from -0.078125 to 0.078125
- norm_gain: float32 [2, 2, 64], replicated, may hold values from 1 to 1.6
- threshold: float32 [], replicated, may hold values from 1 to 2
- cot_img: bfloat16 [6, 1024, 1536], P('shard', ('ctx', 'tp')), may hold values from -6 to 6
- cot_txt: bfloat16 [6, 160, 1536], P('shard', ('ctx', 'tp')), may hold values from -6 to 6
Outputs:
- out_img: bfloat16 [6, 1024, 1536], P('shard', ('ctx', 'tp'))
- out_txt: bfloat16 [6, 160, 1536], P('shard', ('ctx', 'tp'))
- grad_img: float32 [6, 1024, 1536], P('shard', ('ctx', 'tp'))
- grad_txt: float32 [6, 160, 1536], P('shard', ('ctx', 'tp'))
- grad_cond: float32 [6, 1536], P('shard')
- grad_mod: float32 [2, 1536, 6, 1536], P(None, ('shard', 'ctx'), None, 'tp')
- grad_qkv: float32 [2, 3, 1536, 1536], P(None, None, ('shard', 'ctx'), 'tp')
- grad_o: float32 [2, 1536, 1536], P(None, 'tp', ('shard', 'ctx'))
- grad_up: float32 [2, 1536, 6144], P(None, ('shard', 'ctx'), 'tp')
- grad_down: float32 [2, 6144, 1536], P(None, 'tp', ('shard', 'ctx'))
- grad_gain: float32 [2, 2, 64], replicated
- clipped_qk: float32 [2, 2, 1536, 1536], P(None, None, ('shard', 'ctx'), 'tp')
- logit_peaks: float32 [24], P('tp')
The draws below stay inside these ranges and needn't reach their ends.
Inputs may be any that keep to these rules, and one draw needn't show every extreme that they name: lengths: text tokens of a sequence; some sequence has exactly 154.
All inputs are finite; a program needn't handle non-finite values.
Results may differ from the reference program's by a relative error of at most 0.017.
Values may be sent and summed in bfloat16 or wider, within the bound.
No kernel may reach another device: no remote copies, remote signals or barrier semaphores. Data moves between devices by JAX's collectives and lax.ppermute only.
A program may use at most 256 MiB of HBM per device.

```python
import jax
import jax.numpy as jnp
from jax import lax

D = 1536
HEADS = 24
HD = 64
FF = 6144
IMG = 1024
TXT_MAX = 154
TXT_SLOTS = 160
SEQS = 6


def draw_lengths(key, part):
    values = jax.random.randint(key, (SEQS,), TXT_MAX // 2, TXT_MAX + 1)
    chosen = jax.random.randint(jax.random.fold_in(key, 11), (), 0, SEQS)
    values = values.at[chosen].set(TXT_MAX)
    return values.astype(jnp.int32)


def shard_levels(stream_key, dims, shards, least, largest):
    gain, own = 1.0, jax.random.fold_in(stream_key, 6)
    for axis_at, parts in shards:
        draws = jnp.exp(jax.random.uniform(jax.random.fold_in(own, axis_at), (parts,), jnp.float32, least / len(shards), largest / len(shards)))
        gain = gain * jnp.repeat(draws, dims[axis_at] // parts).reshape([-1 if axis == axis_at else 1 for axis in range(len(dims))])
    return gain


def noise(own_key, shape, scale, bound, cuts=(), kind=jnp.bfloat16):
    array = jax.random.normal(own_key, shape, jnp.float32) * scale
    if len(cuts) > 0:
        array = shard_levels(own_key, shape, cuts, -0.22, 0.18) * array
    return jnp.clip(array, min=-bound, max=bound).astype(kind)


def setup_inputs(seed: int = 0) -> dict:
    splits = jax.random.split(jax.random.key(seed), 14)
    return {
        "x_img": noise(splits[0], (SEQS, IMG, D), 1.0, 6.0, ((0, 2), (1, 16))),
        "x_txt": noise(splits[1], (SEQS, TXT_SLOTS, D), 1.0, 6.0, ((0, 2), (1, 16))),
        "cond": noise(splits[2], (SEQS, D), 1.0, 6.0, ((0, 2),)),
        "lengths": draw_lengths(jax.random.fold_in(splits[13], 71), 0),
        "mod_w": noise(splits[4], (2, D, 6, D), D ** -0.5, 0.15625, ((1, 8), (3, 4))),
        "qkv_w": noise(splits[5], (2, 3, D, D), D ** -0.5, 0.15625, ((2, 8), (3, 4))),
        "o_w": noise(splits[6], (2, D, D), (D // 32) ** -0.5, 0.875, ((1, 4), (2, 8))),
        "up_w": noise(splits[7], (2, D, FF), D ** -0.5, 0.15625, ((1, 8), (2, 4))),
        "down_w": noise(splits[8], (2, FF, D), FF ** -0.5, 0.078125, ((1, 4), (2, 8))),
        "norm_gain": jnp.clip(jax.random.uniform(splits[9], (2, 2, HD), jnp.float32, 1.0, 1.6), 1.0, 1.6),
        "threshold": jnp.clip(jax.random.uniform(splits[10], (), jnp.float32, 1.0, 2.0), 1.0, 2.0),
        "cot_img": noise(splits[11], (SEQS, IMG, D), 1.0, 6.0, ((0, 2), (1, 16))),
        "cot_txt": noise(splits[12], (SEQS, TXT_SLOTS, D), 1.0, 6.0, ((0, 2), (1, 16))),
    }


@jax.custom_vjp
def low(v):
    return lax.optimization_barrier(v.astype(jnp.bfloat16)).astype(jnp.float32)

@jax.custom_vjp
def low_back(v):
    return v

def low_keep(v):
    return (low(v), None)

def low_pass(kept, grad):
    return (grad,)

def back_keep(v):
    return (v, None)

def back_low(kept, grad):
    return (low(grad),)
low.defvjp(low_keep, low_pass)
low_back.defvjp(back_keep, back_low)
EPS = 1e-06
QUERY_SCALE = 0.125
HIGHEST_PRECISION = lax.Precision.HIGHEST

def dense_high(left, right):
    return jnp.dot(left, right, precision=HIGHEST_PRECISION, preferred_element_type=jnp.float32)

def layer_norm(values):
    center = values - lax.optimization_barrier(jnp.mean(values, axis=-1, keepdims=True))
    spread = lax.optimization_barrier(jnp.mean(center * center, axis=-1, keepdims=True))
    return center * lax.rsqrt(spread + EPS)

def modulate(values, shift, scale):
    return layer_norm(values) * (1.0 + scale) + shift

def head_norm(values, gain_vec, factor):
    shape_in = values.shape
    split_heads = values.reshape(shape_in[:-1] + (shape_in[-1] // gain_vec.shape[0], gain_vec.shape[0]))
    square = lax.optimization_barrier(jnp.mean(split_heads * split_heads, axis=-1, keepdims=True))
    return (split_heads * lax.rsqrt(square + EPS) * gain_vec * factor).reshape(shape_in)

def head_major(values):
    return values.reshape(values.shape[0], HEADS, HD).transpose(1, 0, 2)

def one_sequence(weights, inputs):
    qkv_w, o_w, up_w, down_w, norm_gain = weights
    x_img, x_txt, modulation, length = inputs
    streams = (x_img, x_txt)
    query_parts = []
    key_parts = []
    value_parts = []
    for stream in range(2):
        first_in = low(modulate(streams[stream], modulation[stream, 0], modulation[stream, 1]))
        query_raw = low_back(dense_high(first_in, qkv_w[stream, 0]))
        key_raw = low_back(dense_high(first_in, qkv_w[stream, 1]))
        value_raw = low_back(dense_high(first_in, qkv_w[stream, 2]))
        query_parts.append(low(head_norm(query_raw, norm_gain[stream, 0], QUERY_SCALE)))
        key_parts.append(low(head_norm(key_raw, norm_gain[stream, 1], 1.0)))
        value_parts.append(low(value_raw))
    queries = jnp.concatenate(query_parts, axis=0)
    keys_all = jnp.concatenate(key_parts, axis=0)
    values_all = jnp.concatenate(value_parts, axis=0)
    key_place = jnp.arange(IMG + TXT_SLOTS, dtype=jnp.int32)
    allowed = (key_place < IMG) | (key_place - IMG < length)

    def attend_head(operands):
        query_head, key_head, value_head = operands
        scores = low_back(jnp.einsum('qd,kd->qk', query_head, key_head, precision=HIGHEST_PRECISION))
        masked = jnp.where(allowed[None, :], scores, -jnp.inf)
        probabilities = jnp.exp(masked - jax.nn.logsumexp(masked, axis=-1, keepdims=True))
        mixed_out = jnp.einsum('qk,kd->qd', low(probabilities), value_head, precision=HIGHEST_PRECISION)
        return (low(low_back(mixed_out)), jnp.max(masked))
    attended, head_peaks = lax.map(jax.checkpoint(attend_head), (head_major(queries), head_major(keys_all), head_major(values_all)))
    attended = attended.transpose(1, 0, 2).reshape(IMG + TXT_SLOTS, D)
    segments = (attended[:IMG], attended[IMG:])
    results = []
    for stream in range(2):
        attn = low_back(dense_high(segments[stream], o_w[stream]))
        mid = streams[stream] + modulation[stream, 2] * attn
        second_in = low(modulate(mid, modulation[stream, 3], modulation[stream, 4]))
        hidden_pre = low_back(dense_high(second_in, up_w[stream]))
        hidden = low(jax.nn.gelu(hidden_pre, approximate=True))
        mlp = low_back(dense_high(hidden, down_w[stream]))
        results.append(mid + modulation[stream, 5] * mlp)
    return ((results[0], results[1]), head_peaks)

def reference(x_img, x_txt, cond, lengths, mod_w, qkv_w, o_w, up_w, down_w, norm_gain, threshold, cot_img, cot_txt):

    def forward(image_in, text_in, cond_in, mod_in, qkv_in, out_in, up_in, down_in, gain_in):
        cond_act = low(jax.nn.silu(cond_in))
        modulation = low_back(jnp.einsum('sd,tdkf->stkf', cond_act, mod_in, precision=HIGHEST_PRECISION))
        weights = (qkv_in, out_in, up_in, down_in, gain_in)

        def per_sequence(carry_zero, inputs):
            outputs, head_peaks = jax.checkpoint(one_sequence)(weights, inputs)
            return (carry_zero, (outputs, head_peaks))
        carry_zero, (outputs, head_peaks) = lax.scan(per_sequence, jnp.float32(0), (image_in, text_in, modulation, lengths))
        return (outputs, lax.optimization_barrier(jnp.max(head_peaks, axis=0)))
    primals = (x_img.astype(jnp.float32), x_txt.astype(jnp.float32), cond.astype(jnp.float32), mod_w.astype(jnp.float32), qkv_w.astype(jnp.float32), o_w.astype(jnp.float32), up_w.astype(jnp.float32), down_w.astype(jnp.float32), norm_gain)
    outputs, backward, logit_peaks = jax.vjp(forward, *primals, has_aux=True)
    grads = backward((cot_img.astype(jnp.float32), cot_txt.astype(jnp.float32)))
    factor = jnp.sqrt(threshold / jnp.maximum(logit_peaks, threshold))
    columns = jnp.repeat(factor, HD)
    clipped = primals[4][:, :2] * columns
    return (outputs[0].astype(jnp.bfloat16), outputs[1].astype(jnp.bfloat16), grads[0], grads[1], grads[2], grads[3], grads[4], grads[5], grads[6], grads[7], grads[8], clipped, logit_peaks)
```

```python
import functools

import jax
import jax.numpy as jnp
from jax import lax
from jax.experimental import pallas as pl
from jax.experimental.pallas import tpu as pltpu
from jax.sharding import Mesh, PartitionSpec as P

EPS = 1e-06
QUERY_SCALE = 0.125
BF16 = jnp.bfloat16
F32 = jnp.float32
MASKED = -1e30


def layer_norm(values):
    center = values - jnp.mean(values, axis=-1, keepdims=True)
    spread = jnp.mean(center * center, axis=-1, keepdims=True)
    return center * lax.rsqrt(spread + EPS)


def modulate(values, shift, scale):
    return layer_norm(values) * (1.0 + scale) + shift


def gelu_tanh(values):
    return jax.nn.gelu(values, approximate=True)


def trade(values, axis):
    return lax.ppermute(values, axis, [(0, 1), (1, 0)])


def cross(values):
    return lax.ppermute(values, ("l", "c"), [(0, 0), (1, 2), (2, 1), (3, 3)])


def feature_order(width, shard_count):
    place = jnp.arange(width, dtype=jnp.int32)
    block = width // (shard_count * 4)
    inner = place % block
    h = (place // block) % 2 ^ lax.axis_index("h")
    s = (place // (2 * block)) % shard_count
    if shard_count == 2:
        s = s ^ lax.axis_index("s")
    low = place // (2 * block * shard_count) ^ lax.axis_index("c")
    return ((s * 2 + h) * 2 + low) * block + inner


def one_hot(source):
    width = source.shape[0]
    rows = lax.broadcasted_iota(jnp.int32, (width, width), 0)
    return (rows == source[None, :]).astype(BF16)


def permute_exact(values, matrix, dims):
    high = lax.reduce_precision(values, 8, 7)
    rest = values - high
    middle = lax.reduce_precision(rest, 8, 7)
    low = rest - middle
    parts = [
        lax.dot_general(part.astype(BF16), matrix, (dims, ((), ())), preferred_element_type=F32)
        for part in (high, middle, low)
    ]
    return parts[0] + (parts[1] + parts[2])


def gather_weight(shard, shard_count):
    own = cross(shard)
    pair = jnp.concatenate([own, trade(own, "h")], axis=1)
    if shard_count == 2:
        near = jnp.concatenate([pair, trade(pair, "s")], axis=1)
    else:
        near = lax.all_gather(pair, "s", axis=1, tiled=True)
    return near, trade(near, "c")


def scatter_grad(near, far, shard_count):
    total = near + trade(far, "c").astype(F32)
    half = total.shape[1] // 2
    if shard_count == 2:
        moved = trade(total[:, half:].astype(BF16), "s")
        total = total[:, :half] + moved.astype(F32)
    else:
        total = lax.psum_scatter(total, "s", scatter_dimension=1, tiled=True)
    half = total.shape[1] // 2
    moved = trade(total[:, half:].astype(BF16), "h")
    total = total[:, :half] + moved.astype(F32)
    return cross(total.astype(BF16)).astype(F32)


def gather_rows(image, text):
    half = image.shape[1] // 2
    rows = image.shape[0]
    both = jnp.concatenate([image, text], axis=0)
    first, second = both[:, :half], both[:, half:]
    first_pair = jnp.stack([first, trade(first, "y")])
    second_pair = jnp.stack([second, trade(second, "l")])
    first_far = trade(first_pair, "l")
    second_far = trade(second_pair, "y")
    near = [first_pair[0], first_pair[1], first_far[1], first_far[0]]
    far = [second_pair[0], second_far[0], second_far[1], second_pair[1]]
    return [
        (
            jnp.concatenate([block[:rows] for block in blocks], axis=0),
            jnp.concatenate([block[rows:] for block in blocks], axis=0),
        )
        for blocks in (near, far)
    ]


def reduce_rows(near, far):
    def blocks(pair, which):
        image, text = pair
        rows_i, rows_t = image.shape[0] // 4, text.shape[0] // 4
        return jnp.stack(
            [
                jnp.concatenate(
                    [image[k * rows_i : (k + 1) * rows_i], text[k * rows_t : (k + 1) * rows_t]]
                )
                for k in which
            ]
        )

    rows_i = near[0].shape[0] // 4
    first_in = trade(blocks(near, (2, 3)).astype(BF16), "l").astype(F32)
    second_in = trade(blocks(far, (1, 2)).astype(BF16), "y").astype(F32)
    first_keep = blocks(near, (0, 1))
    second_keep = blocks(far, (0, 3))
    first_last = trade((first_keep[1] + first_in[0]).astype(BF16), "y")
    second_last = trade((second_keep[1] + second_in[1]).astype(BF16), "l")
    first = first_keep[0] + first_in[1] + first_last.astype(F32)
    second = second_keep[0] + second_in[0] + second_last.astype(F32)
    total = jnp.concatenate([first, second], axis=1)
    return total[:rows_i], total[rows_i:]


def head_mean(values, head_dim):
    width = values.shape[-1]
    rows = lax.broadcasted_iota(jnp.int32, (width, width), 0) // head_dim
    cols = lax.broadcasted_iota(jnp.int32, (width, width), 1) // head_dim
    spread = jnp.where(rows == cols, 1.0 / head_dim, 0.0).astype(BF16)
    high = lax.reduce_precision(values, 8, 7)
    low = (values - high).astype(BF16)
    return jnp.dot(high.astype(BF16), spread, preferred_element_type=F32) + jnp.dot(
        low, spread, preferred_element_type=F32
    )


def two_sided(pair, weights, form):
    return jnp.einsum(form, pair[0], weights[0], preferred_element_type=F32) + jnp.einsum(
        form, pair[1], weights[1], preferred_element_type=F32
    )


def sequence_rows(ref, seq, sizes):
    img, txt, seqs = sizes
    parts = [ref[pl.ds(pl.multiple_of((b * seqs + seq) * img, 16), img), :] for b in range(4)]
    base = 4 * seqs * img
    parts += [
        ref[pl.ds(pl.multiple_of(base + (b * seqs + seq) * txt, 16), txt), :] for b in range(4)
    ]
    return jnp.concatenate(parts, axis=0)


def store_rows(ref, seq, sizes, value):
    img, txt, seqs = sizes
    base = 4 * seqs * img
    for b in range(4):
        ref[pl.ds(pl.multiple_of((b * seqs + seq) * img, 16), img), :] = value[
            b * img : (b + 1) * img
        ]
        ref[pl.ds(pl.multiple_of(base + (b * seqs + seq) * txt, 16), txt), :] = value[
            4 * img + b * txt : 4 * img + (b + 1) * txt
        ]


def both_heads(rows, head_dim):
    lane = lax.broadcasted_iota(jnp.int32, rows.shape, 1)
    zero = jnp.zeros_like(rows)
    return jnp.concatenate(
        [jnp.where(lane < head_dim, rows, zero), jnp.where(lane >= head_dim, rows, zero)], axis=0
    )


def join_heads(stacked, head_dim):
    count = stacked.shape[0] // 2
    lane = lax.broadcasted_iota(jnp.int32, (count, stacked.shape[1]), 1)
    return jnp.where(lane < head_dim, stacked[:count], stacked[count:])


NT = (((1,), (1,)), ((), ()))
TN = (((0,), (0,)), ((), ()))
NN = (((1,), (0,)), ((), ()))


def attend_kernel(sizes, head_dim, *refs):
    q_ref, k_refs, v_refs = refs[0], refs[1:5], refs[5:9]
    bias_ref, out_ref, norm_ref, peak_ref = refs[9:]
    seq = pl.program_id(1)
    query = both_heads(sequence_rows(q_ref, seq, sizes), head_dim)
    keys = jnp.concatenate([sequence_rows(r, seq, sizes) for r in k_refs], axis=0)
    values = jnp.concatenate([sequence_rows(r, seq, sizes) for r in v_refs], axis=0)
    scores = lax.dot_general(keys, query, NT, preferred_element_type=F32) + bias_ref[0]
    highest = jnp.max(scores, axis=0, keepdims=True)
    weights = jnp.exp(scores - highest)
    total = jnp.sum(weights, axis=0, keepdims=True)
    mixed = lax.dot_general(values, weights.astype(BF16), TN, preferred_element_type=F32)
    mixed = jnp.transpose(mixed * (1.0 / total))
    store_rows(out_ref, seq, sizes, join_heads(mixed, head_dim).astype(BF16))
    norm_ref[0] = highest + jnp.log(total)
    peak_ref[0] = highest


def attend_back_kernel(sizes, head_dim, *refs):
    q_ref, k_refs, v_refs = refs[0], refs[1:5], refs[5:9]
    bias_ref, norm_ref, grad_ref = refs[9:12]
    gq_ref, gk_refs, gv_refs = refs[12], refs[13:17], refs[17:21]
    seq = pl.program_id(1)
    query = both_heads(sequence_rows(q_ref, seq, sizes), head_dim)
    grad = both_heads(sequence_rows(grad_ref, seq, sizes), head_dim)
    keys = jnp.concatenate([sequence_rows(r, seq, sizes) for r in k_refs], axis=0)
    values = jnp.concatenate([sequence_rows(r, seq, sizes) for r in v_refs], axis=0)
    scores = lax.dot_general(keys, query, NT, preferred_element_type=F32) + bias_ref[0]
    probs = jnp.exp(scores - norm_ref[0])
    grad_probs = lax.dot_general(values, grad, NT, preferred_element_type=F32)
    inner = jnp.sum(probs * grad_probs, axis=0, keepdims=True)
    grad_scores = (probs * (grad_probs - inner)).astype(BF16)
    grad_values = lax.dot_general(probs.astype(BF16), grad, NN, preferred_element_type=F32)
    grad_keys = lax.dot_general(grad_scores, query, NN, preferred_element_type=F32)
    grad_query = lax.dot_general(keys, grad_scores, TN, preferred_element_type=F32)
    store_rows(gq_ref, seq, sizes, join_heads(jnp.transpose(grad_query), head_dim))
    count = keys.shape[0] // 4
    for j in range(4):
        store_rows(gk_refs[j], seq, sizes, grad_keys[j * count : (j + 1) * count].astype(BF16))
        store_rows(gv_refs[j], seq, sizes, grad_values[j * count : (j + 1) * count].astype(BF16))


def attention_specs(rows, seqs, keys, pair_count):
    q_spec = pl.BlockSpec((rows, 128), lambda p, s: (0, p))
    k_specs = [pl.BlockSpec((rows, 128), lambda p, s: (0, p)) for _ in range(4)]
    v_specs = [pl.BlockSpec((rows, 128), lambda p, s: (0, pair_count + p)) for _ in range(4)]
    bias_spec = pl.BlockSpec((1, keys, 1), lambda p, s: (s, 0, 0))
    return q_spec, k_specs, v_specs, bias_spec


def attend(queries, key_values, bias, sizes, head_dim):
    rows, width = queries.shape
    seqs, keys = bias.shape[0], bias.shape[1]
    pairs = width // 128
    lanes = 2 * (keys // 4)
    q_spec, k_specs, v_specs, bias_spec = attention_specs(rows, seqs, keys, pairs)
    line = pl.BlockSpec((1, 1, lanes), lambda p, s: (p * seqs + s, 0, 0))
    return pl.pallas_call(
        functools.partial(attend_kernel, sizes, head_dim),
        grid=(pairs, seqs),
        in_specs=[q_spec, *k_specs, *v_specs, bias_spec],
        out_specs=[q_spec, line, line],
        out_shape=[
            jax.ShapeDtypeStruct((rows, width), BF16),
            jax.ShapeDtypeStruct((pairs * seqs, 1, lanes), F32),
            jax.ShapeDtypeStruct((pairs * seqs, 1, lanes), F32),
        ],
        cost_estimate=pl.CostEstimate(
            flops=pairs * seqs * keys * lanes * 128 * 4,
            bytes_accessed=rows * width * 20,
            transcendentals=pairs * seqs * keys * lanes,
        ),
        compiler_params=pltpu.CompilerParams(vmem_limit_bytes=60 << 20),
    )(queries, *key_values, *key_values, bias)


def attend_back(queries, key_values, bias, norms, grads, sizes, head_dim):
    rows, width = queries.shape
    seqs, keys = bias.shape[0], bias.shape[1]
    pairs = width // 128
    lanes = 2 * (keys // 4)
    q_spec, k_specs, v_specs, bias_spec = attention_specs(rows, seqs, keys, pairs)
    line = pl.BlockSpec((1, 1, lanes), lambda p, s: (p * seqs + s, 0, 0))
    out = pl.pallas_call(
        functools.partial(attend_back_kernel, sizes, head_dim),
        grid=(pairs, seqs),
        in_specs=[q_spec, *k_specs, *v_specs, bias_spec, line, q_spec],
        out_specs=[q_spec] * 9,
        out_shape=[jax.ShapeDtypeStruct((rows, width), F32)]
        + [jax.ShapeDtypeStruct((rows, width), BF16)] * 8,
        cost_estimate=pl.CostEstimate(
            flops=pairs * seqs * keys * lanes * 128 * 10,
            bytes_accessed=rows * width * 40,
            transcendentals=pairs * seqs * keys * lanes,
        ),
        compiler_params=pltpu.CompilerParams(vmem_limit_bytes=60 << 20),
    )(queries, *key_values, *key_values, bias, norms, grads)
    return out[0], out[1:5], out[5:9]


def local(
    x_img,
    x_txt,
    cond,
    lengths,
    mod_w,
    qkv_w,
    o_w,
    up_w,
    down_w,
    norm_gain,
    threshold,
    cot_img,
    cot_txt,
):
    shard_count = lax.axis_size("s")
    head_dim = norm_gain.shape[2]
    seqs, img_rows, width = x_img.shape
    txt_real = x_txt.shape[1]
    txt_rows = -(-txt_real // 16) * 16
    sizes = (img_rows, txt_rows, seqs)
    shapes = ((seqs, img_rows, width), (seqs, txt_rows, width))
    feat = mod_w.shape[3]
    block = mod_w.shape[1]
    heads = qkv_w.shape[3] // head_dim
    own = {name: lax.axis_index(name) for name in ("s", "h", "l", "y", "c")}

    weights = {
        "qkv": gather_weight(qkv_w.reshape(6, block, -1), shard_count),
        "o": gather_weight(jnp.swapaxes(o_w, 1, 2), shard_count),
        "up": gather_weight(up_w, shard_count),
        "down": gather_weight(jnp.swapaxes(down_w, 1, 2), shard_count),
    }

    source = feature_order(width, shard_count)
    order = one_hot(source)

    def pad_text(values):
        return jnp.pad(values, ((0, 0), (0, txt_rows - txt_real), (0, 0)))

    def arrange(image, text):
        both = jnp.concatenate(
            [image.reshape(-1, width), pad_text(text).reshape(-1, width)], axis=0
        )
        moved = jnp.dot(both, order, preferred_element_type=F32)
        count = seqs * img_rows
        return [moved[:count].reshape(shapes[0]), moved[count:].reshape(shapes[1])]

    inputs = arrange(x_img, x_txt)
    grad_out = arrange(cot_img, cot_txt)

    cond_float = cond.astype(F32)
    cond_act = jax.nn.silu(cond_float).astype(BF16)
    cond_all = lax.all_gather(cond_act, "s", axis=0, tiled=True)
    cond_rows = lax.dynamic_index_in_dim(
        cond_all.reshape(cond_all.shape[0], -1, block),
        (own["s"] * 2 + own["h"]) * 2 + own["l"],
        axis=1,
        keepdims=False,
    )
    mod_part = jnp.einsum("sd,tdkf->stkf", cond_rows, mod_w, preferred_element_type=F32)
    if shard_count == 2:
        mine = lax.dynamic_slice_in_dim(mod_part, own["s"] * seqs, seqs, axis=0)
        other = lax.dynamic_slice_in_dim(mod_part, (1 - own["s"]) * seqs, seqs, axis=0)
        mod_sum = mine + trade(other, "s")
    else:
        mod_sum = lax.psum_scatter(mod_part, "s", scatter_dimension=0, tiled=True)
    mod_sum = mod_sum + trade(mod_sum, "h")
    mod_sum = mod_sum + trade(mod_sum, "l")
    mod_full = lax.all_gather(mod_sum, ("y", "c"), axis=3, tiled=True)
    modulation = permute_exact(mod_full.reshape(-1, width), order, ((1,), (0,))).reshape(
        seqs, 2, 6, width
    )

    def entry(stream, index):
        return modulation[:, stream, index][:, None, :]

    def flat(pair):
        return [v.reshape(-1, width) for v in pair]

    def unflat(pair):
        return [v.reshape(shape) for v, shape in zip(pair, shapes)]

    first_low = [modulate(inputs[s], entry(s, 0), entry(s, 1)).astype(BF16) for s in range(2)]
    first_near, first_far = gather_rows(*flat(first_low))
    qkv_near, qkv_far = weights["qkv"]
    projected = []
    for s in range(2):
        pair = (first_near[s], first_far[s])
        projected.append(
            [
                two_sided(pair, (qkv_near[3 * s + c], qkv_far[3 * s + c]), "rd,df->rf")
                for c in range(3)
            ]
        )
    scales = (QUERY_SCALE, 1.0)
    roots = [
        [lax.rsqrt(head_mean(projected[s][c] * projected[s][c], head_dim) + EPS) for c in range(2)]
        for s in range(2)
    ]
    gains = [[jnp.tile(norm_gain[s, c], heads) * scales[c] for c in range(2)] for s in range(2)]
    normed = [
        [(projected[s][c] * roots[s][c] * gains[s][c]).astype(BF16) for c in range(2)]
        for s in range(2)
    ]
    queries = jnp.concatenate([normed[0][0], normed[1][0]], axis=0)
    own_kv = jnp.concatenate(
        [
            jnp.concatenate([normed[s][1], projected[s][2].astype(BF16)], axis=1)
            for s in range(2)
        ],
        axis=0,
    )
    h_kv = trade(own_kv, "h")
    key_values = [own_kv, trade(own_kv, "c"), h_kv, trade(h_kv, "c")]

    text_bias = []
    for jh, jc in ((0, 0), (0, 1), (1, 0), (1, 1)):
        member = [jnp.zeros((seqs, 4 * img_rows), F32)]
        for jy, jl in ((0, 0), (1, 0), (1, 1), (0, 1)):
            ctx_at = (own["h"] ^ jh) * 2 + (own["l"] ^ jl)
            tp_at = (own["y"] ^ jy) * 2 + (own["c"] ^ jc)
            row = jnp.arange(txt_rows, dtype=jnp.int32)
            slot = (ctx_at * 4 + tp_at) * txt_real + row
            allowed = (row < txt_real)[None, :] & (slot[None, :] < lengths[:, None])
            member.append(jnp.where(allowed, 0.0, MASKED))
        text_bias.append(jnp.concatenate(member, axis=1))
    bias = jnp.concatenate(text_bias, axis=1)[:, :, None]

    attended, log_norm, highest = attend(queries, key_values, bias, sizes, head_dim)
    count_i = 4 * seqs * img_rows
    attended_s = (attended[:count_i], attended[count_i:])
    o_near, o_far = weights["o"]
    attn_out = unflat(
        reduce_rows(
            *[
                [
                    jnp.einsum("rf,df->rd", attended_s[s], w[s], preferred_element_type=F32)
                    for s in range(2)
                ]
                for w in (o_near, o_far)
            ]
        )
    )
    mid = [inputs[s] + entry(s, 2) * attn_out[s] for s in range(2)]
    second_low = [modulate(mid[s], entry(s, 3), entry(s, 4)).astype(BF16) for s in range(2)]
    second_near, second_far = gather_rows(*flat(second_low))
    up_near, up_far = weights["up"]
    down_near, down_far = weights["down"]
    hidden_pre = [
        two_sided((second_near[s], second_far[s]), (up_near[s], up_far[s]), "rd,df->rf")
        for s in range(2)
    ]
    hidden_low = [gelu_tanh(hidden_pre[s]).astype(BF16) for s in range(2)]

    mlp_grad_low = [(grad_out[s] * entry(s, 5)).astype(BF16) for s in range(2)]
    mlp_near, mlp_far = gather_rows(*flat(mlp_grad_low))
    pre_grad = []
    for s in range(2):
        hidden_back = two_sided((mlp_near[s], mlp_far[s]), (down_near[s], down_far[s]), "rd,df->rf")
        unused, gelu_vjp = jax.vjp(gelu_tanh, hidden_pre[s])
        pre_grad.append(gelu_vjp(hidden_back)[0].astype(BF16))
    second_grad = unflat(
        reduce_rows(
            *[
                [
                    jnp.einsum("rf,df->rd", pre_grad[s], w[s], preferred_element_type=F32)
                    for s in range(2)
                ]
                for w in (up_near, up_far)
            ]
        )
    )
    mlp_out = unflat(
        reduce_rows(
            *[
                [
                    jnp.einsum("rf,df->rd", hidden_low[s], w[s], preferred_element_type=F32)
                    for s in range(2)
                ]
                for w in (down_near, down_far)
            ]
        )
    )
    results = [(mid[s] + entry(s, 5) * mlp_out[s]).astype(BF16) for s in range(2)]
    gate_two = [jnp.sum(grad_out[s] * mlp_out[s], axis=1) for s in range(2)]

    def weight_grad(left_near, left_far, right):
        near, far = [
            jnp.stack(
                [
                    jnp.einsum("rd,rf->df", left[s], right[s], preferred_element_type=F32)
                    for s in range(2)
                ]
            )
            for left in (left_near, left_far)
        ]
        return scatter_grad(near, far.astype(BF16), shard_count)

    grad_down = weight_grad(mlp_near, mlp_far, hidden_low)
    grad_up = weight_grad(second_near, second_far, pre_grad)

    mid_grad = []
    shift_two = []
    scale_two = []
    for s in range(2):
        unused, mod_vjp = jax.vjp(modulate, mid[s], entry(s, 3), entry(s, 4))
        mid_part, shift_part, scale_part = mod_vjp(second_grad[s])
        mid_grad.append(grad_out[s] + mid_part)
        shift_two.append(shift_part[:, 0])
        scale_two.append(scale_part[:, 0])
    attn_grad_low = [(mid_grad[s] * entry(s, 2)).astype(BF16) for s in range(2)]
    gate_one = [jnp.sum(mid_grad[s] * attn_out[s], axis=1) for s in range(2)]
    attn_near, attn_far = gather_rows(*flat(attn_grad_low))
    grad_o = weight_grad(attn_near, attn_far, attended_s)
    mixed_grad = jnp.concatenate(
        [
            two_sided((attn_near[s], attn_far[s]), (o_near[s], o_far[s]), "rd,df->rf")
            for s in range(2)
        ],
        axis=0,
    ).astype(BF16)
    query_sum, key_grads, value_grads = attend_back(
        queries, key_values, bias, log_norm, mixed_grad, sizes, head_dim
    )

    kv_grads = [jnp.concatenate([key_grads[j], value_grads[j]], axis=1) for j in range(4)]
    own_sum = kv_grads[0].astype(F32) + trade(kv_grads[1], "c").astype(F32)
    h_sum = kv_grads[2].astype(F32) + trade(kv_grads[3], "c").astype(F32)
    kv_sum = own_sum + trade(h_sum.astype(BF16), "h").astype(F32)
    inner_width = queries.shape[1]
    key_sum, value_sum = kv_sum[:, :inner_width], kv_sum[:, inner_width:]

    bounds = ((0, count_i), (count_i, queries.shape[0]))
    qkv_near_parts, qkv_far_parts = [], []
    first_near_parts, first_far_parts = [], []
    gain_terms = []
    for s in range(2):
        start, stop = bounds[s]
        grads = []
        gain_pair = []
        for c, grad_sum in ((0, query_sum), (1, key_sum)):
            grad = grad_sum[start:stop]
            unit = projected[s][c] * roots[s][c]
            gain_pair.append(
                jnp.sum(jnp.sum(grad * unit, axis=0).reshape(heads, head_dim), axis=0) * scales[c]
            )
            scaled = grad * gains[s][c]
            grads.append(roots[s][c] * (scaled - unit * head_mean(scaled * unit, head_dim)))
        grads.append(value_sum[start:stop])
        low = [g.astype(BF16) for g in grads]
        gain_terms.append(jnp.stack(gain_pair))
        for c in range(3):
            for parts, left in ((qkv_near_parts, first_near), (qkv_far_parts, first_far)):
                parts.append(jnp.einsum("rd,rf->df", left[s], low[c], preferred_element_type=F32))
        for parts, w in ((first_near_parts, qkv_near), (first_far_parts, qkv_far)):
            parts.append(
                sum(
                    jnp.einsum("rf,df->rd", low[c], w[3 * s + c], preferred_element_type=F32)
                    for c in range(3)
                )
            )
    grad_qkv = scatter_grad(
        jnp.stack(qkv_near_parts), jnp.stack(qkv_far_parts).astype(BF16), shard_count
    ).reshape(qkv_w.shape)
    first_grad = unflat(reduce_rows(first_near_parts, first_far_parts))

    input_grads = []
    mod_terms = []
    for s in range(2):
        unused, mod_vjp = jax.vjp(modulate, inputs[s], entry(s, 0), entry(s, 1))
        input_part, shift_part, scale_part = mod_vjp(first_grad[s])
        input_grads.append(mid_grad[s] + input_part)
        mod_terms.append(
            jnp.stack(
                [
                    shift_part[:, 0],
                    scale_part[:, 0],
                    gate_one[s],
                    shift_two[s],
                    scale_two[s],
                    gate_two[s],
                ],
                axis=1,
            )
        )

    back = ((1,), (1,))

    def restore(pair, dtype):
        both = jnp.concatenate(flat(pair), axis=0)
        if dtype == BF16:
            moved = lax.dot_general(both, order, (back, ((), ())), preferred_element_type=BF16)
        else:
            moved = permute_exact(both, order, back)
        count = seqs * img_rows
        return (
            moved[:count].reshape(shapes[0]),
            moved[count:].reshape(shapes[1])[:, :txt_real],
        )

    out_img, out_txt = restore(results, BF16)
    grad_img, grad_txt = restore(input_grads, F32)

    mod_low = jnp.stack(mod_terms).astype(BF16).reshape(-1, width)
    mod_low = lax.dot_general(mod_low, order, (back, ((), ())), preferred_element_type=BF16)
    mod_grad = lax.psum(mod_low, ("h", "l", "y", "c")).astype(F32).reshape(2, seqs, 6, width)
    own_mod = lax.dynamic_slice_in_dim(
        mod_grad, (own["y"] * 2 + own["c"]) * feat, feat, axis=3
    ).astype(BF16)
    mod_seqs = lax.all_gather(own_mod, "s", axis=1, tiled=True)
    grad_mod = jnp.einsum("sd,tskf->tdkf", cond_rows, mod_seqs, preferred_element_type=F32)
    cond_part = jnp.einsum("tskf,tdkf->sd", mod_seqs, mod_w, preferred_element_type=F32)
    cond_part = lax.psum(cond_part, ("y", "c"))
    cond_cols = lax.all_gather(cond_part, ("s", "h", "l"), axis=1, tiled=True)
    cond_total = lax.dynamic_slice_in_dim(cond_cols, own["s"] * seqs, seqs, axis=0)
    unused, silu_vjp = jax.vjp(jax.nn.silu, cond_float)
    grad_cond = silu_vjp(cond_total)[0]

    gain_grad = lax.psum(jnp.stack(gain_terms), ("s", "h", "l", "y", "c"))

    lanes = highest.shape[2] // 2
    row = jnp.arange(lanes, dtype=jnp.int32)
    valid = (row < 4 * img_rows) | ((row - 4 * img_rows) % txt_rows < txt_real)
    tops = highest.reshape(-1, seqs, 2, lanes)
    tops = jnp.max(jnp.where(valid, tops, -jnp.inf), axis=(1, 3)).reshape(heads)
    slots = jnp.where(jnp.arange(2)[:, None] == own["l"], tops[None, :], -jnp.inf)
    slots = lax.pmax(slots, ("s", "h", "l", "c"))
    peaks = lax.dynamic_index_in_dim(slots, own["c"], axis=0, keepdims=False)
    factor = jnp.sqrt(threshold / jnp.maximum(peaks, threshold))
    columns = jnp.repeat(factor, head_dim)
    clipped = qkv_w[:, :2].astype(F32) * columns
    return (
        out_img,
        out_txt,
        grad_img,
        grad_txt,
        grad_cond,
        grad_mod,
        grad_qkv,
        jnp.swapaxes(grad_o, 1, 2),
        grad_up,
        jnp.swapaxes(grad_down, 1, 2),
        gain_grad,
        clipped,
        peaks,
    )


def solution(mesh):
    shard, ctx, tp = (mesh.shape[name] for name in ("shard", "ctx", "tp"))
    fine = Mesh(mesh.devices.reshape(shard, ctx // 2, 2, tp // 2, 2), ("s", "h", "l", "y", "c"))
    ctx_axes, tp_axes = ("h", "l"), ("y", "c")
    rows = P("s", ctx_axes + tp_axes, None)
    weight = ("s",) + ctx_axes
    mod = P(None, weight, None, tp_axes)
    qkv = P(None, None, weight, tp_axes)
    inward = P(None, tp_axes, weight)
    outward = P(None, weight, tp_axes)
    return jax.shard_map(
        local,
        mesh=fine,
        in_specs=(
            rows,
            rows,
            P("s", None),
            P("s"),
            mod,
            qkv,
            inward,
            outward,
            inward,
            P(),
            P(),
            rows,
            rows,
        ),
        out_specs=(
            rows,
            rows,
            rows,
            rows,
            P("s", None),
            mod,
            qkv,
            inward,
            outward,
            inward,
            P(),
            qkv,
            P(tp_axes),
        ),
        check_vma=False,
    )
```

```python
import functools

import jax
import jax.numpy as jnp
from jax import lax
from jax.experimental import pallas as pl
from jax.experimental.pallas import tpu as pltpu
from jax.sharding import Mesh, PartitionSpec as P

EPS = 1e-06
QUERY_SCALE = 0.125
BF16 = jnp.bfloat16
F32 = jnp.float32
MASKED = -1e30
NT = (((1,), (1,)), ((), ()))
TN = (((0,), (0,)), ((), ()))
NN = (((1,), (0,)), ((), ()))


def trade(values, axis):
    return lax.ppermute(values, axis, [(0, 1), (1, 0)])


def cross(values):
    moved = lax.ppermute(values, ("l", "c"), [(1, 2), (2, 1)])
    return jnp.where(lax.axis_index("l") == lax.axis_index("c"), values, moved)


def in_order(values, axis, dim):
    other = trade(values, axis)
    first = lax.axis_index(axis) == 0
    return jnp.concatenate(
        [jnp.where(first, values, other), jnp.where(first, other, values)], axis=dim
    )


def total_over(values, axes):
    for axis in axes:
        values = values + trade(values, axis)
    return values


def highest_over(values, axes):
    for axis in axes:
        values = jnp.maximum(values, trade(values, axis))
    return values


def after(values, others):
    return lax.optimization_barrier((values, others))[0]


def feature_order(width, shard_count):
    place = jnp.arange(width, dtype=jnp.int32)
    block = width // (shard_count * 4)
    member = place // block
    low = member // (shard_count * 2) ^ lax.axis_index("c")
    return (member % (shard_count * 2) * 2 + low) * block + place % block


def one_hot(source):
    width = source.shape[0]
    rows = lax.broadcasted_iota(jnp.int32, (width, width), 0)
    return (rows == source[None, :]).astype(BF16)


def permute_exact(values, matrix, dims):
    high = lax.reduce_precision(values, 8, 7)
    rest = values - high
    middle = lax.reduce_precision(rest, 8, 7)
    low = rest - middle
    parts = [
        lax.dot_general(part.astype(BF16), matrix, (dims, ((), ())), preferred_element_type=F32)
        for part in (high, middle, low)
    ]
    return parts[0] + (parts[1] + parts[2])


def gather_weight(shard, others=None):
    own = cross(shard)
    if others is not None:
        own = after(own, others)
    return lax.all_gather(own, ("s", "h"), axis=1, tiled=True)


def dot(left, right, dims):
    return lax.dot_general(left, right, dims, preferred_element_type=F32)


def row_groups(sizes):
    img, txt, seqs = sizes
    base = seqs * img
    groups = [(s * img, (s + 1) * img, 0, s) for s in range(seqs)]
    return groups + [(base + s * txt, base + (s + 1) * txt, 1, s) for s in range(seqs)]


def stream_parts(sizes, stream):
    img, txt, seqs = sizes
    per = seqs * (img + txt)
    lo, hi = ((0, seqs * img), (seqs * img, per))[stream]
    return [(b * per + lo, b * per + hi) for b in range(4)]


def stream_rows(ref, sizes, stream):
    return jnp.concatenate([ref[a:b, :] for a, b in stream_parts(sizes, stream)], axis=0)


def put_stream(ref, sizes, stream, value):
    at = 0
    for a, b in stream_parts(sizes, stream):
        ref[a:b, :] = value[at : at + b - a].astype(ref.dtype)
        at += b - a


def vec(ref, stream, seq, k):
    row = (seq * 2 + stream) * 6 + k
    return ref[row : row + 1, :]


def normal(values):
    center = values - jnp.mean(values, axis=-1, keepdims=True)
    inv = lax.rsqrt(jnp.mean(center * center, axis=-1, keepdims=True) + EPS)
    return center * inv, inv


def normal_back(grad, unit, inv):
    mean = jnp.mean(grad, axis=-1, keepdims=True)
    return inv * (grad - mean - unit * jnp.mean(grad * unit, axis=-1, keepdims=True))


def put_halves(near_ref, far_ref, a, b, value):
    half = value.shape[1] // 2
    near_ref[a:b, :] = value[:, :half].astype(near_ref.dtype)
    far_ref[a:b, :] = value[:, half:].astype(far_ref.dtype)


def first_kernel(sizes, x_ref, cot_ref, mod_ref, n1_ref, f1_ref, n2_ref, f2_ref):
    for a, b, t, s in row_groups(sizes):
        unit, _ = normal(x_ref[a:b, :].astype(F32))
        put_halves(n1_ref, f1_ref, a, b, unit * (1.0 + vec(mod_ref, t, s, 1)) + vec(mod_ref, t, s, 0))
        put_halves(n2_ref, f2_ref, a, b, cot_ref[a:b, :].astype(F32) * vec(mod_ref, t, s, 5))


def middle_kernel(sizes, x_ref, attn_ref, mod_ref, mid_ref, n_ref, f_ref):
    for a, b, t, s in row_groups(sizes):
        mid = x_ref[a:b, :].astype(F32) + vec(mod_ref, t, s, 2) * attn_ref[a:b, :]
        mid_ref[a:b, :] = mid
        unit, _ = normal(mid)
        put_halves(n_ref, f_ref, a, b, unit * (1.0 + vec(mod_ref, t, s, 4)) + vec(mod_ref, t, s, 3))


def last_kernel(sizes, mid_ref, mlp_ref, cot_ref, mod_ref, out_ref, sum_ref):
    for a, b, t, s in row_groups(sizes):
        mlp = mlp_ref[a:b, :]
        out_ref[a:b, :] = (mid_ref[a:b, :] + vec(mod_ref, t, s, 5) * mlp).astype(BF16)
        row = t * sizes[2] + s
        sum_ref[row : row + 1, :] = jnp.sum(
            cot_ref[a:b, :].astype(F32) * mlp, axis=0, keepdims=True
        )


def middle_back_kernel(
    sizes, mid_ref, cot_ref, grad_ref, attn_ref, mod_ref, out_ref, n_ref, f_ref, sum_ref
):
    count = 2 * sizes[2]
    for a, b, t, s in row_groups(sizes):
        row = t * sizes[2] + s
        unit, inv = normal(mid_ref[a:b, :])
        grad = grad_ref[a:b, :]
        sum_ref[row : row + 1, :] = jnp.sum(grad, axis=0, keepdims=True)
        sum_ref[count + row : count + row + 1, :] = jnp.sum(grad * unit, axis=0, keepdims=True)
        back = normal_back(grad * (1.0 + vec(mod_ref, t, s, 4)), unit, inv)
        total = cot_ref[a:b, :].astype(F32) + back
        out_ref[a:b, :] = total
        put_halves(n_ref, f_ref, a, b, total * vec(mod_ref, t, s, 2))
        sum_ref[2 * count + row : 2 * count + row + 1, :] = jnp.sum(
            total * attn_ref[a:b, :], axis=0, keepdims=True
        )


def first_back_kernel(sizes, x_ref, mid_grad_ref, grad_ref, mod_ref, out_ref, sum_ref):
    count = 2 * sizes[2]
    for a, b, t, s in row_groups(sizes):
        row = t * sizes[2] + s
        unit, inv = normal(x_ref[a:b, :].astype(F32))
        grad = grad_ref[a:b, :]
        sum_ref[row : row + 1, :] = jnp.sum(grad, axis=0, keepdims=True)
        sum_ref[count + row : count + row + 1, :] = jnp.sum(grad * unit, axis=0, keepdims=True)
        back = normal_back(grad * (1.0 + vec(mod_ref, t, s, 1)), unit, inv)
        out_ref[a:b, :] = mid_grad_ref[a:b, :] + back


def call(kernel, outs, *args, flops=1 << 20):
    return pl.pallas_call(
        kernel,
        out_shape=[jax.ShapeDtypeStruct(shape, dtype) for shape, dtype in outs],
        cost_estimate=pl.CostEstimate(flops=flops, bytes_accessed=1 << 20, transcendentals=0),
        compiler_params=pltpu.CompilerParams(vmem_limit_bytes=48 << 20),
    )(*args)


def head_spread(width, head_dim):
    rows = lax.broadcasted_iota(jnp.int32, (width, width), 0) // head_dim
    cols = lax.broadcasted_iota(jnp.int32, (width, width), 1) // head_dim
    return jnp.where(rows == cols, 1.0 / head_dim, 0.0).astype(BF16)


def head_mean(values, spread):
    high = values.astype(BF16)
    low = (values - high.astype(F32)).astype(BF16)
    return dot(high, spread, NN) + dot(low, spread, NN)


def qkv_kernel(sizes, head_dim, near_ref, far_ref, wn_ref, wf_ref, gain_ref, q_ref, kv_ref, raw_ref):
    spread = head_spread(q_ref.shape[1], head_dim)

    def part(c):
        for t in range(2):
            left = stream_rows(near_ref, sizes, t), stream_rows(far_ref, sizes, t)
            total = dot(left[0], wn_ref[t, 0], NN) + dot(left[1], wf_ref[t, 0], NN)
            if c < 2:
                put_stream(raw_ref.at[0], sizes, t, total)
                root = lax.rsqrt(head_mean(total * total, spread) + EPS)
                total = total * root * gain_ref[2 * t + c : 2 * t + c + 1, :]
            put_stream(q_ref if c == 0 else kv_ref.at[0], sizes, t, total)

    for c in range(3):
        pl.when(pl.program_id(0) == c)(functools.partial(part, c))


def qkv_project(near, far, w_near, w_far, gains, sizes, head_dim):
    rows, half = near.shape
    width = gains.shape[1]
    whole = pl.BlockSpec((rows, half), lambda c: (0, 0))
    weight = pl.BlockSpec((2, 1, half, width), lambda c: (0, c, 0, 0))
    return pl.pallas_call(
        functools.partial(qkv_kernel, sizes, head_dim),
        grid=(3,),
        in_specs=[whole, whole, weight, weight, pl.BlockSpec((4, width), lambda c: (0, 0))],
        out_specs=[
            pl.BlockSpec((rows, width), lambda c: (0, 0)),
            pl.BlockSpec((1, rows, width), lambda c: (jnp.maximum(c - 1, 0), 0, 0)),
            pl.BlockSpec((1, rows, width), lambda c: (jnp.minimum(c, 1), 0, 0)),
        ],
        out_shape=[
            jax.ShapeDtypeStruct((rows, width), BF16),
            jax.ShapeDtypeStruct((2, rows, width), BF16),
            jax.ShapeDtypeStruct((2, rows, width), F32),
        ],
        cost_estimate=pl.CostEstimate(flops=1 << 20, bytes_accessed=1 << 20, transcendentals=0),
        compiler_params=pltpu.CompilerParams(vmem_limit_bytes=48 << 20),
    )(
        near,
        far,
        w_near.reshape(2, 3, half, width),
        w_far.reshape(2, 3, half, width),
        gains,
    )


def qkv_back_kernel(
    sizes, head_dim, q_ref, own_ref, c_ref, h_ref, raw_ref, gain_ref, low_ref, sum_ref
):
    width = q_ref.shape[1]
    spread = head_spread(width, head_dim)
    for t in range(2):
        for c in range(2):
            gain = gain_ref[2 * t + c : 2 * t + c + 1, :]
            total = jnp.zeros((1, width), F32)
            for a, b in stream_parts(sizes, t):
                if c == 0:
                    grad = q_ref[a:b, :]
                else:
                    grad = own_ref[0, a:b, :].astype(F32) + c_ref[0, a:b, :].astype(F32)
                    grad = grad + h_ref[0, a:b, :].astype(F32)
                raw = raw_ref[c, a:b, :]
                root = lax.rsqrt(head_mean(raw * raw, spread) + EPS)
                unit = raw * root
                total = total + jnp.sum(grad * unit, axis=0, keepdims=True)
                scaled = grad * gain
                back = root * (scaled - unit * head_mean(scaled * unit, spread))
                low_ref[a:b, c * width : (c + 1) * width] = back.astype(BF16)
            sum_ref[2 * t + c : 2 * t + c + 1, :] = total
        for a, b in stream_parts(sizes, t):
            grad = own_ref[1, a:b, :].astype(F32) + c_ref[1, a:b, :].astype(F32)
            low_ref[a:b, 2 * width :] = (grad + h_ref[1, a:b, :].astype(F32)).astype(BF16)


def mixed_kernel(sizes, near_ref, far_ref, wn_ref, wf_ref, out_ref):
    for t in range(2):
        total = dot(stream_rows(near_ref, sizes, t), wn_ref[t], NN)
        total = total + dot(stream_rows(far_ref, sizes, t), wf_ref[t], NN)
        put_stream(out_ref, sizes, t, total)


GELU_ROOT = 0.7978845608028654
GELU_CUBE = 0.044715


def mlp_kernel(sizes, sn_ref, sf_ref, mn_ref, mf_ref, un_ref, uf_ref, dn_ref, df_ref, h_ref, g_ref):
    for t in range(2):
        pre = dot(stream_rows(sn_ref, sizes, t), un_ref[t], NN)
        pre = pre + dot(stream_rows(sf_ref, sizes, t), uf_ref[t], NN)
        square = pre * pre
        bent = jnp.tanh(GELU_ROOT * pre * (1.0 + GELU_CUBE * square))
        half = 0.5 * (1.0 + bent)
        put_stream(h_ref, sizes, t, pre * half)
        back = dot(stream_rows(mn_ref, sizes, t), dn_ref[t], NN)
        back = back + dot(stream_rows(mf_ref, sizes, t), df_ref[t], NN)
        slope = half + 0.5 * pre * (1.0 - bent * bent) * (
            GELU_ROOT * (1.0 + 3.0 * GELU_CUBE * square)
        )
        put_stream(g_ref, sizes, t, back * slope)


def mlp(second, cot, up, down, sizes):
    rows, half = second[0].shape
    width = up[0].shape[2]
    tile = 384 if width % 384 == 0 else width
    whole = pl.BlockSpec((rows, half), lambda j: (0, 0))
    weight = pl.BlockSpec((2, half, tile), lambda j: (0, 0, j))
    out = pl.BlockSpec((rows, tile), lambda j: (0, j))
    return pl.pallas_call(
        functools.partial(mlp_kernel, sizes),
        grid=(width // tile,),
        in_specs=[whole] * 4 + [weight] * 4,
        out_specs=[out] * 2,
        out_shape=[jax.ShapeDtypeStruct((rows, width), BF16)] * 2,
        cost_estimate=pl.CostEstimate(flops=1 << 20, bytes_accessed=1 << 20, transcendentals=0),
        compiler_params=pltpu.CompilerParams(vmem_limit_bytes=56 << 20),
    )(*second, *cot, *up, *down)


SENT = ((2, 3), (1, 2))
KEPT = ((0, 1), (0, 3))


def project_kernel(sizes, rows_ref, *refs):
    weights, outs = refs[:2], refs[2:]
    per = rows_ref.shape[0] // 4
    for t in range(2):
        left = stream_rows(rows_ref, sizes, t)
        lo, hi = stream_parts(sizes, t)[0]
        for side in range(2):
            chunks = weights[side].shape[0] // 2
            depth = weights[side].shape[2]
            total = dot(left[:, :depth], weights[side][t * chunks], NT)
            for c in range(1, chunks):
                total = total + dot(
                    left[:, c * depth : (c + 1) * depth], weights[side][t * chunks + c], NT
                )
            count = hi - lo
            for k in range(2):
                b = SENT[side][k]
                outs[2 * side][k, lo:hi, :] = total[b * count : (b + 1) * count].astype(BF16)
                b = KEPT[side][k]
                outs[2 * side + 1][k, lo:hi, :] = total[b * count : (b + 1) * count]


def project(rows, near, far, sizes):
    count, depth = rows.shape
    chunks, half, inner = near.shape
    tile = 384 if half % 384 == 0 else half
    weight = pl.BlockSpec((chunks, tile, inner), lambda j: (0, j, 0))
    out = pl.BlockSpec((2, count // 4, tile), lambda j: (0, 0, j))
    shape = (2, count // 4, half)
    return pl.pallas_call(
        functools.partial(project_kernel, sizes),
        grid=(half // tile,),
        in_specs=[pl.BlockSpec((count, depth), lambda j: (0, 0)), weight, weight],
        out_specs=[out] * 4,
        out_shape=[jax.ShapeDtypeStruct(shape, d) for d in (BF16, F32, BF16, F32)],
        cost_estimate=pl.CostEstimate(flops=1 << 20, bytes_accessed=1 << 20, transcendentals=0),
        compiler_params=pltpu.CompilerParams(vmem_limit_bytes=56 << 20),
    )(rows, near, far)


def grad_kernel(sizes, add, left_ref, right_ref, *refs):
    for t in range(2):
        total = dot(stream_rows(left_ref, sizes, t), stream_rows(right_ref, sizes, t), TN)
        if add:
            total = total + refs[0][t].reshape(total.shape).astype(F32)
        refs[-1][t] = total.astype(BF16).reshape(refs[-1].shape[1:])


def stream_grads(left, right, sizes, split, other=None):
    rows, depth = left.shape
    width = right.shape[1]
    tile = 384 if width % 384 == 0 else width
    if split:
        out = pl.BlockSpec((2, 1, depth, tile), lambda j: (0, j, 0, 0))
        shape = (2, width // tile, depth, tile)
    else:
        out = pl.BlockSpec((2, depth, tile), lambda j: (0, 0, j))
        shape = (2, depth, width)
    extra = [] if other is None else [other]
    return pl.pallas_call(
        functools.partial(grad_kernel, sizes, bool(extra)),
        grid=(width // tile,),
        in_specs=[
            pl.BlockSpec((rows, depth), lambda j: (0, 0)),
            pl.BlockSpec((rows, tile), lambda j: (0, j)),
        ]
        + [out] * len(extra),
        out_specs=out,
        out_shape=jax.ShapeDtypeStruct(shape, BF16),
        cost_estimate=pl.CostEstimate(flops=1 << 20, bytes_accessed=1 << 20, transcendentals=0),
        compiler_params=pltpu.CompilerParams(vmem_limit_bytes=48 << 20),
    )(left, right, *extra)


def pair_grad(left, right, sizes, split=False):
    far = trade(stream_grads(left[1], right, sizes, split), "c")
    return stream_grads(left[0], right, sizes, split, far)


def shard_grad(total):
    return lax.psum_scatter(total, ("s", "h"), scatter_dimension=total.ndim - 2, tiled=True)


def own_grad(block):
    return cross(block).astype(F32)


def gather_rows(first, second):
    first_pair = jnp.stack([first, trade(first, "y")])
    second_pair = jnp.stack([second, trade(second, "l")])
    first_far = trade(first_pair, "l")
    second_far = trade(second_pair, "y")
    near = [first_pair[0], first_pair[1], first_far[1], first_far[0]]
    far = [second_pair[0], second_far[0], second_far[1], second_pair[1]]
    return jnp.concatenate(near), jnp.concatenate(far)


def reduce_rows(near_send, near_keep, far_send, far_keep):
    first_in = trade(near_send, "l")
    second_in = trade(far_send, "y")
    first_last = trade((near_keep[1] + first_in[0].astype(F32)).astype(BF16), "y")
    second_last = trade((far_keep[1] + second_in[1].astype(F32)).astype(BF16), "l")
    first = near_keep[0] + first_in[1].astype(F32) + first_last.astype(F32)
    second = far_keep[0] + second_in[0].astype(F32) + second_last.astype(F32)
    return jnp.concatenate([first, second], axis=1), (first_in, second_in)


def sequence_places(seq, sizes):
    img, txt, seqs = sizes
    per = seqs * (img + txt)
    places = [(pl.multiple_of(b * per + seq * img, 16), img) for b in range(4)]
    return places + [(pl.multiple_of(b * per + seqs * img + seq * txt, 16), txt) for b in range(4)]


def sequence_rows(ref, seq, sizes):
    return jnp.concatenate([ref[pl.ds(a, n), :] for a, n in sequence_places(seq, sizes)], axis=0)


def store_rows(ref, seq, sizes, value):
    at = 0
    for a, n in sequence_places(seq, sizes):
        ref[pl.ds(a, n), :] = value[at : at + n]
        at += n


def both_heads(rows, head_dim):
    lane = lax.broadcasted_iota(jnp.int32, rows.shape, 1)
    zero = jnp.zeros_like(rows)
    return jnp.concatenate(
        [jnp.where(lane < head_dim, rows, zero), jnp.where(lane >= head_dim, rows, zero)], axis=0
    )


def join_heads(stacked, head_dim):
    count = stacked.shape[0] // 2
    lane = lax.broadcasted_iota(jnp.int32, (count, stacked.shape[1]), 1)
    return jnp.where(lane < head_dim, stacked[:count], stacked[count:])


def attend_kernel(sizes, head_dim, *refs):
    q_ref, kv_refs = refs[0], refs[1:5]
    bias_ref, out_ref, norm_ref, peak_ref = refs[5:]
    seq = pl.program_id(1)
    query = both_heads(sequence_rows(q_ref, seq, sizes), head_dim)
    keys = jnp.concatenate([sequence_rows(r.at[0], seq, sizes) for r in kv_refs], axis=0)
    values = jnp.concatenate([sequence_rows(r.at[1], seq, sizes) for r in kv_refs], axis=0)
    scores = lax.dot_general(keys, query, NT, preferred_element_type=F32) + bias_ref[0]
    highest = jnp.max(scores, axis=0, keepdims=True)
    weights = jnp.exp(scores - highest)
    total = jnp.sum(weights, axis=0, keepdims=True)
    mixed = lax.dot_general(values, weights.astype(BF16), TN, preferred_element_type=F32)
    mixed = jnp.transpose(mixed * (1.0 / total))
    store_rows(out_ref, seq, sizes, join_heads(mixed, head_dim).astype(BF16))
    norm_ref[0] = highest + jnp.log(total)
    peak_ref[0] = highest


def attend_back_kernel(sizes, head_dim, *refs):
    q_ref, kv_refs = refs[0], refs[1:5]
    bias_ref, norm_ref, grad_ref = refs[5:8]
    gq_ref, gkv_refs = refs[8], refs[9:13]
    seq = pl.program_id(1)
    query = both_heads(sequence_rows(q_ref, seq, sizes), head_dim)
    grad = both_heads(sequence_rows(grad_ref, seq, sizes), head_dim)
    keys = jnp.concatenate([sequence_rows(r.at[0], seq, sizes) for r in kv_refs], axis=0)
    values = jnp.concatenate([sequence_rows(r.at[1], seq, sizes) for r in kv_refs], axis=0)
    scores = lax.dot_general(keys, query, NT, preferred_element_type=F32) + bias_ref[0]
    probs = jnp.exp(scores - norm_ref[0])
    grad_probs = lax.dot_general(values, grad, NT, preferred_element_type=F32)
    inner = jnp.sum(probs * grad_probs, axis=0, keepdims=True)
    grad_scores = (probs * (grad_probs - inner)).astype(BF16)
    grad_values = lax.dot_general(probs.astype(BF16), grad, NN, preferred_element_type=F32)
    grad_keys = lax.dot_general(grad_scores, query, NN, preferred_element_type=F32)
    grad_query = lax.dot_general(keys, grad_scores, TN, preferred_element_type=F32)
    store_rows(gq_ref, seq, sizes, join_heads(jnp.transpose(grad_query), head_dim))
    count = keys.shape[0] // 4
    for j in range(4):
        part = slice(j * count, (j + 1) * count)
        store_rows(gkv_refs[j].at[0], seq, sizes, grad_keys[part].astype(BF16))
        store_rows(gkv_refs[j].at[1], seq, sizes, grad_values[part].astype(BF16))


def attention_specs(rows, keys):
    q_spec = pl.BlockSpec((rows, 128), lambda p, s: (0, p))
    kv_specs = [pl.BlockSpec((2, rows, 128), lambda p, s: (0, 0, p)) for _ in range(4)]
    bias_spec = pl.BlockSpec((1, keys, 1), lambda p, s: (s, 0, 0))
    return q_spec, kv_specs, bias_spec


def attend(queries, key_values, bias, sizes, head_dim):
    rows, width = queries.shape
    seqs, keys = bias.shape[0], bias.shape[1]
    pairs = width // 128
    lanes = 2 * (keys // 4)
    q_spec, kv_specs, bias_spec = attention_specs(rows, keys)
    line = pl.BlockSpec((1, 1, lanes), lambda p, s: (p * seqs + s, 0, 0))
    return pl.pallas_call(
        functools.partial(attend_kernel, sizes, head_dim),
        grid=(pairs, seqs),
        in_specs=[q_spec, *kv_specs, bias_spec],
        out_specs=[q_spec, line, line],
        out_shape=[
            jax.ShapeDtypeStruct((rows, width), BF16),
            jax.ShapeDtypeStruct((pairs * seqs, 1, lanes), F32),
            jax.ShapeDtypeStruct((pairs * seqs, 1, lanes), F32),
        ],
        cost_estimate=pl.CostEstimate(
            flops=pairs * seqs * keys * lanes, bytes_accessed=rows * width, transcendentals=0
        ),
        compiler_params=pltpu.CompilerParams(vmem_limit_bytes=60 << 20),
    )(queries, *key_values, bias)


def attend_back(queries, key_values, bias, norms, grads, sizes, head_dim):
    rows, width = queries.shape
    seqs, keys = bias.shape[0], bias.shape[1]
    pairs = width // 128
    lanes = 2 * (keys // 4)
    q_spec, kv_specs, bias_spec = attention_specs(rows, keys)
    line = pl.BlockSpec((1, 1, lanes), lambda p, s: (p * seqs + s, 0, 0))
    out = pl.pallas_call(
        functools.partial(attend_back_kernel, sizes, head_dim),
        grid=(pairs, seqs),
        in_specs=[q_spec, *kv_specs, bias_spec, line, q_spec],
        out_specs=[q_spec, *kv_specs],
        out_shape=[jax.ShapeDtypeStruct((rows, width), F32)]
        + [jax.ShapeDtypeStruct((2, rows, width), BF16)] * 4,
        cost_estimate=pl.CostEstimate(
            flops=pairs * seqs * keys * lanes, bytes_accessed=rows * width, transcendentals=0
        ),
        compiler_params=pltpu.CompilerParams(vmem_limit_bytes=60 << 20),
    )(queries, *key_values, bias, norms, grads)
    return out[0], out[1:]


def local(
    x_img,
    x_txt,
    cond,
    lengths,
    mod_w,
    qkv_w,
    o_w,
    up_w,
    down_w,
    norm_gain,
    threshold,
    cot_img,
    cot_txt,
):
    shard_count = lax.axis_size("s")
    head_dim = norm_gain.shape[2]
    seqs, img_rows, width = x_img.shape
    txt_real = x_txt.shape[1]
    txt_rows = -(-txt_real // 16) * 16
    sizes = (img_rows, txt_rows, seqs)
    per = seqs * (img_rows + txt_rows)
    feat = mod_w.shape[3]
    block = mod_w.shape[1]
    heads = qkv_w.shape[3] // head_dim
    own = {name: lax.axis_index(name) for name in ("s", "h", "l", "y", "c")}

    source = feature_order(width, shard_count)
    order = one_hot(source)
    count_i = seqs * img_rows

    def arrange(image, text):
        text = jnp.pad(text, ((0, 0), (0, txt_rows - txt_real), (0, 0)))
        both = jnp.concatenate([image.reshape(-1, width), text.reshape(-1, width)], axis=0)
        return jnp.dot(both, order, preferred_element_type=BF16)

    inputs, cot = arrange(x_img, x_txt), arrange(cot_img, cot_txt)

    cond_float = cond.astype(F32)
    cond_act = jax.nn.silu(cond_float).astype(BF16)
    if shard_count == 2:
        cond_all = jnp.concatenate([cond_act, trade(cond_act, "s")], axis=0)
    else:
        cond_all = lax.all_gather(cond_act, "s", axis=0, tiled=True)
    cond_rows = lax.dynamic_index_in_dim(
        cond_all.reshape(cond_all.shape[0], -1, block),
        (own["s"] * 2 + own["h"]) * 2 + own["l"],
        axis=1,
        keepdims=False,
    )
    mod_part = jnp.einsum("sd,tdkf->stkf", cond_rows, mod_w, preferred_element_type=F32)
    if shard_count == 2:
        mod_sum = mod_part[:seqs] + trade(mod_part[seqs:], "s")
    else:
        mod_sum = lax.psum_scatter(mod_part, "s", scatter_dimension=0, tiled=True)
    mod_sum = total_over(mod_sum.reshape(seqs * 12, feat), ("h", "l"))
    mod_full = in_order(in_order(mod_sum, "c", 1), "y", 1)
    modulation = permute_exact(mod_full, order, ((1,), (0,)))

    half = width // 2
    halves = [((per, half), BF16)] * 2
    first_n, first_f, mlp_n, mlp_f = call(
        functools.partial(first_kernel, sizes), halves * 2, inputs, cot, modulation
    )
    first = gather_rows(first_n, first_f)
    cot_rows = gather_rows(mlp_n, mlp_f)
    qkv_near = gather_weight(after(qkv_w.reshape(6, block, -1), mod_sum))
    qkv_far = trade(after(qkv_near, first), "c")
    up_near = gather_weight(after(up_w, first))
    scales = jnp.array([QUERY_SCALE, 1.0], F32)
    gains = jnp.tile(norm_gain * scales[None, :, None], (1, 1, heads)).reshape(4, -1)
    queries, own_kv, raw = qkv_project(*first, qkv_near, qkv_far, gains, sizes, head_dim)
    o_near = gather_weight(after(jnp.swapaxes(o_w, 1, 2), first), own_kv)
    h_kv = trade(own_kv, "h")
    down_near = gather_weight(after(jnp.swapaxes(down_w, 1, 2), own_kv), h_kv)
    o_far = trade(after(o_near, h_kv), "c")
    key_values = [own_kv, trade(own_kv, "c"), h_kv, trade(h_kv, "c")]

    text_bias = []
    for jh, jc in ((0, 0), (0, 1), (1, 0), (1, 1)):
        member = [jnp.zeros((seqs, 4 * img_rows), F32)]
        for jy, jl in ((0, 0), (1, 0), (1, 1), (0, 1)):
            ctx_at = (own["h"] ^ jh) * 2 + (own["l"] ^ jl)
            tp_at = (own["y"] ^ jy) * 2 + (own["c"] ^ jc)
            row = jnp.arange(txt_rows, dtype=jnp.int32)
            slot = (ctx_at * 4 + tp_at) * txt_real + row
            allowed = (row < txt_real)[None, :] & (slot[None, :] < lengths[:, None])
            member.append(jnp.where(allowed, 0.0, MASKED))
        text_bias.append(jnp.concatenate(member, axis=1))
    bias = jnp.concatenate(text_bias, axis=1)[:, :, None]

    attended, log_norm, highest = attend(queries, key_values, bias, sizes, head_dim)
    attn_out, _ = reduce_rows(*project(attended, o_near, o_far, sizes))
    mid, second_n, second_f = call(
        functools.partial(middle_kernel, sizes),
        [((per, width), F32), *halves],
        inputs,
        attn_out,
        modulation,
    )
    second = gather_rows(second_n, second_f)
    up_far = trade(after(up_near, second_n), "c")
    down_far = trade(after(down_near, second), "c")
    hidden, pre_grad = mlp(second, cot_rows, (up_near, up_far), (down_near, down_far), sizes)

    second_parts = project(pre_grad, up_near, up_far, sizes)
    hidden, pre_grad = after((hidden, pre_grad), second_parts)
    down_far_grad = stream_grads(cot_rows[1], hidden, sizes, False)
    up_far_grad = stream_grads(second[1], after(pre_grad, down_far_grad), sizes, False)
    hidden = after(hidden, up_far_grad)
    down_total = stream_grads(cot_rows[0], hidden, sizes, False, trade(down_far_grad, "c"))
    up_total = stream_grads(second[0], pre_grad, sizes, False, trade(up_far_grad, "c"))
    second_grad, arrived = reduce_rows(*second_parts)
    down_shard = shard_grad(after(down_total, arrived))
    up_shard = shard_grad(after(up_total, arrived))
    mid_grad, attn_n, attn_f, two_sums = call(
        functools.partial(middle_back_kernel, sizes),
        [((per, width), F32), *halves, ((6 * seqs, width), F32)],
        mid,
        cot,
        second_grad,
        attn_out,
        modulation,
    )
    attn_rows = gather_rows(attn_n, attn_f)
    (mixed_grad,) = call(
        functools.partial(mixed_kernel, sizes),
        [(attended.shape, BF16)],
        *attn_rows,
        o_near,
        o_far,
    )
    mixed_grad = after(mixed_grad, (down_total, up_total))
    query_sum, kv_grads = attend_back(
        queries, key_values, bias, log_norm, mixed_grad, sizes, head_dim
    )
    h_low = (kv_grads[2].astype(F32) + trade(kv_grads[3], "c").astype(F32)).astype(BF16)
    h_grads = trade(h_low, "h")
    c_grads = trade(kv_grads[1], "c")

    mlp_out, _ = reduce_rows(*project(after(hidden, h_low), down_near, down_far, sizes))
    results, gate_sums = call(
        functools.partial(last_kernel, sizes),
        [((per, width), BF16), ((2 * seqs, width), F32)],
        mid,
        mlp_out,
        cot,
        modulation,
    )
    o_total = pair_grad(attn_rows, after(attended, query_sum), sizes)
    grad_down, grad_up = own_grad(down_shard), own_grad(up_shard)
    grad_o = own_grad(shard_grad(after(o_total, up_shard)))

    low_all, gain_sums = call(
        functools.partial(qkv_back_kernel, sizes, head_dim),
        [((4 * per, 3 * heads * head_dim), BF16), (gains.shape, F32)],
        after(query_sum, (mlp_out, o_total)),
        kv_grads[0],
        c_grads,
        h_grads,
        raw,
        gains,
    )
    gain_terms = jnp.sum(gain_sums.reshape(2, 2, heads, head_dim), axis=2) * scales[None, :, None]
    low_all = after(low_all, (grad_down, grad_up, mlp_out))
    grad_qkv = own_grad(shard_grad(pair_grad(first, low_all, sizes, True)))
    first_grad, _ = reduce_rows(*project(low_all, qkv_near, qkv_far, sizes))
    input_grads, one_sums = call(
        functools.partial(first_back_kernel, sizes),
        [((per, width), F32), ((4 * seqs, width), F32)],
        inputs,
        mid_grad,
        first_grad,
        modulation,
    )

    back = ((1,), (1,))

    def restore(moved):
        return (
            moved[:count_i].reshape(seqs, img_rows, width),
            moved[count_i:].reshape(seqs, txt_rows, width)[:, :txt_real],
        )

    out_img, out_txt = restore(
        lax.dot_general(results, order, (back, ((), ())), preferred_element_type=BF16)
    )
    grad_img, grad_txt = restore(permute_exact(input_grads, order, back))

    lanes = highest.shape[2] // 2
    row = jnp.arange(lanes, dtype=jnp.int32)
    valid = (row < 4 * img_rows) | ((row - 4 * img_rows) % txt_rows < txt_real)
    tops = highest.reshape(-1, seqs, 2, lanes)
    tops = jnp.max(jnp.where(valid, tops, -jnp.inf), axis=(1, 3)).reshape(1, heads)
    places = jnp.arange(4 * heads)[None, :] // heads
    tops = jnp.where(places == own["y"] * 2 + own["l"], jnp.tile(tops, (1, 4)), MASKED)

    count = 2 * seqs
    mod_low = jnp.concatenate(
        [one_sums, two_sums[2 * count :], two_sums[: 2 * count], gate_sums], axis=0
    ).astype(BF16)
    mod_count = mod_low.shape[0]
    mod_low = lax.dot_general(mod_low, order, (back, ((), ())), preferred_element_type=F32)
    extra = [gain_terms.reshape(1, -1), tops]
    extra = jnp.concatenate([jnp.pad(e, ((0, 0), (0, feat - e.shape[1]))) for e in extra])
    extra = jnp.pad(extra, ((0, -(mod_count + 2) % 8), (0, 0)))
    mod_low = jnp.concatenate([mod_low, jnp.tile(extra, (1, width // feat))], axis=0)
    is_top = jnp.arange(mod_low.shape[0])[:, None] == mod_count + 1

    def join(first, second):
        return jnp.where(is_top, jnp.maximum(first, second), first + second)

    quarters = [mod_low[:, k * feat : (k + 1) * feat] for k in range(width // feat)]
    at_c, at_y = own["c"] == 0, own["y"] == 0
    keep = [jnp.where(at_c, quarters[2 * k], quarters[2 * k + 1]) for k in range(2)]
    send = [jnp.where(at_c, quarters[2 * k + 1], quarters[2 * k]) for k in range(2)]
    pair = join(jnp.stack(keep), trade(jnp.stack(send), "c"))
    mod_sum = join(
        jnp.where(at_y, pair[0], pair[1]), trade(jnp.where(at_y, pair[1], pair[0]), "y")
    )
    for axis in ("l", "h"):
        mod_sum = join(mod_sum, trade(mod_sum, axis))
    if shard_count == 2:
        mod_members = jnp.stack([mod_sum, trade(mod_sum, "s")])
    else:
        mod_members = lax.all_gather(mod_sum, "s")
    gain_grad = jnp.sum(mod_members[:, mod_count], axis=0)[: 4 * head_dim]
    gain_grad = gain_grad.reshape(norm_gain.shape)
    tops = jnp.max(mod_members[:, mod_count + 1], axis=0)[: 4 * heads]
    peaks = lax.dynamic_slice_in_dim(tops, (own["y"] * 2 + own["c"]) * heads, heads)
    mod_seqs = mod_members[:, :mod_count].astype(BF16).reshape(-1, 6, 2, seqs, feat)
    mod_seqs = mod_seqs.transpose(2, 0, 3, 1, 4).reshape(2, -1, 6, feat)
    grad_mod = jnp.einsum("sd,tskf->tdkf", cond_rows, mod_seqs, preferred_element_type=F32)
    cond_part = jnp.einsum("tskf,tdkf->sd", mod_seqs, mod_w, preferred_element_type=F32)
    cond_part = in_order(in_order(total_over(cond_part, ("c", "y")), "l", 1), "h", 1)
    if shard_count == 2:
        mine, other = cond_part[:seqs], trade(cond_part[seqs:], "s")
        at_s = own["s"] == 0
        cond_total = jnp.concatenate(
            [jnp.where(at_s, mine, other), jnp.where(at_s, other, mine)], axis=1
        )
    else:
        cond_cols = lax.all_gather(cond_part, "s", axis=1, tiled=True)
        cond_total = lax.dynamic_slice_in_dim(cond_cols, own["s"] * seqs, seqs, axis=0)
    unused, silu_vjp = jax.vjp(jax.nn.silu, cond_float)
    grad_cond = silu_vjp(cond_total)[0]

    factor = jnp.sqrt(threshold / jnp.maximum(peaks, threshold))
    columns = jnp.repeat(factor, head_dim)
    clipped = qkv_w[:, :2].astype(F32) * columns
    return (
        out_img,
        out_txt,
        grad_img,
        grad_txt,
        grad_cond,
        grad_mod,
        grad_qkv,
        jnp.swapaxes(grad_o, 1, 2),
        grad_up,
        jnp.swapaxes(grad_down, 1, 2),
        gain_grad,
        clipped,
        peaks,
    )


def solution(mesh):
    shard, ctx, tp = (mesh.shape[name] for name in ("shard", "ctx", "tp"))
    fine = Mesh(mesh.devices.reshape(shard, ctx // 2, 2, tp // 2, 2), ("s", "h", "l", "y", "c"))
    ctx_axes, tp_axes = ("h", "l"), ("y", "c")
    rows = P("s", ctx_axes + tp_axes, None)
    weight = ("s",) + ctx_axes
    mod = P(None, weight, None, tp_axes)
    qkv = P(None, None, weight, tp_axes)
    inward = P(None, tp_axes, weight)
    outward = P(None, weight, tp_axes)
    return jax.shard_map(
        local,
        mesh=fine,
        in_specs=(
            rows,
            rows,
            P("s", None),
            P("s"),
            mod,
            qkv,
            inward,
            outward,
            inward,
            P(),
            P(),
            rows,
            rows,
        ),
        out_specs=(
            rows,
            rows,
            rows,
            rows,
            P("s", None),
            mod,
            qkv,
            inward,
            outward,
            inward,
            P(),
            qkv,
            P(tp_axes),
        ),
        check_vma=False,
    )
```

```python
import functools

import jax
import jax.numpy as jnp
from jax import lax
from jax.experimental import pallas as pl
from jax.experimental.pallas import tpu as pltpu
from jax.sharding import Mesh, PartitionSpec as P

EPS = 1e-06
QUERY_SCALE = 0.125
BF16 = jnp.bfloat16
F32 = jnp.float32
MASKED = -1e30
NT = (((1,), (1,)), ((), ()))
TN = (((0,), (0,)), ((), ()))
NN = (((1,), (0,)), ((), ()))


def trade(values, axis):
    return lax.ppermute(values, axis, [(0, 1), (1, 0)])


def cross(values):
    moved = lax.ppermute(values, ("l", "c"), [(1, 2), (2, 1)])
    return jnp.where(lax.axis_index("l") == lax.axis_index("c"), values, moved)


def in_order(values, axis, dim):
    other = trade(values, axis)
    first = lax.axis_index(axis) == 0
    return jnp.concatenate(
        [jnp.where(first, values, other), jnp.where(first, other, values)], axis=dim
    )


def total_over(values, axes):
    for axis in axes:
        values = values + trade(values, axis)
    return values


def highest_over(values, axes):
    for axis in axes:
        values = jnp.maximum(values, trade(values, axis))
    return values


def after(values, others):
    return lax.optimization_barrier((values, others))[0]


def feature_order(width, shard_count):
    place = jnp.arange(width, dtype=jnp.int32)
    block = width // (shard_count * 4)
    member = place // block
    low = member // (shard_count * 2) ^ lax.axis_index("c")
    return (member % (shard_count * 2) * 2 + low) * block + place % block


def one_hot(source):
    width = source.shape[0]
    rows = lax.broadcasted_iota(jnp.int32, (width, width), 0)
    return (rows == source[None, :]).astype(BF16)


def permute_exact(values, matrix, dims):
    high = lax.reduce_precision(values, 8, 7)
    rest = values - high
    middle = lax.reduce_precision(rest, 8, 7)
    low = rest - middle
    parts = [
        lax.dot_general(part.astype(BF16), matrix, (dims, ((), ())), preferred_element_type=F32)
        for part in (high, middle, low)
    ]
    return parts[0] + (parts[1] + parts[2])


def gather_weight(shard, others=None):
    own = cross(shard)
    if others is not None:
        own = after(own, others)
    return lax.all_gather(own, ("s", "h"), axis=1, tiled=True)


def dot(left, right, dims):
    return lax.dot_general(left, right, dims, preferred_element_type=F32)


def row_groups(sizes):
    img, txt, seqs = sizes
    base = seqs * img
    groups = [(s * img, (s + 1) * img, 0, s) for s in range(seqs)]
    return groups + [(base + s * txt, base + (s + 1) * txt, 1, s) for s in range(seqs)]


def stream_parts(sizes, stream):
    img, txt, seqs = sizes
    per = seqs * (img + txt)
    lo, hi = ((0, seqs * img), (seqs * img, per))[stream]
    return [(b * per + lo, b * per + hi) for b in range(4)]


def stream_rows(ref, sizes, stream):
    return jnp.concatenate([ref[a:b, :] for a, b in stream_parts(sizes, stream)], axis=0)


def put_stream(ref, sizes, stream, value):
    at = 0
    for a, b in stream_parts(sizes, stream):
        ref[a:b, :] = value[at : at + b - a].astype(ref.dtype)
        at += b - a


def vec(ref, stream, seq, k):
    row = (seq * 2 + stream) * 6 + k
    return ref[row : row + 1, :]


def normal(values):
    center = values - jnp.mean(values, axis=-1, keepdims=True)
    inv = lax.rsqrt(jnp.mean(center * center, axis=-1, keepdims=True) + EPS)
    return center * inv, inv


def normal_back(grad, unit, inv):
    mean = jnp.mean(grad, axis=-1, keepdims=True)
    return inv * (grad - mean - unit * jnp.mean(grad * unit, axis=-1, keepdims=True))


def put_halves(near_ref, far_ref, a, b, value):
    half = value.shape[1] // 2
    near_ref[a:b, :] = value[:, :half].astype(near_ref.dtype)
    far_ref[a:b, :] = value[:, half:].astype(far_ref.dtype)


def first_kernel(sizes, x_ref, cot_ref, mod_ref, n1_ref, f1_ref, n2_ref, f2_ref):
    for a, b, t, s in row_groups(sizes):
        unit, _ = normal(x_ref[a:b, :].astype(F32))
        put_halves(n1_ref, f1_ref, a, b, unit * (1.0 + vec(mod_ref, t, s, 1)) + vec(mod_ref, t, s, 0))
        put_halves(n2_ref, f2_ref, a, b, cot_ref[a:b, :].astype(F32) * vec(mod_ref, t, s, 5))


def middle_kernel(sizes, x_ref, attn_ref, mod_ref, mid_ref, n_ref, f_ref):
    for a, b, t, s in row_groups(sizes):
        mid = x_ref[a:b, :].astype(F32) + vec(mod_ref, t, s, 2) * attn_ref[a:b, :]
        mid_ref[a:b, :] = mid
        unit, _ = normal(mid)
        put_halves(n_ref, f_ref, a, b, unit * (1.0 + vec(mod_ref, t, s, 4)) + vec(mod_ref, t, s, 3))


def last_kernel(sizes, mid_ref, mlp_ref, cot_ref, mod_ref, out_ref, sum_ref):
    for a, b, t, s in row_groups(sizes):
        mlp = mlp_ref[a:b, :]
        out_ref[a:b, :] = (mid_ref[a:b, :] + vec(mod_ref, t, s, 5) * mlp).astype(BF16)
        row = t * sizes[2] + s
        sum_ref[row : row + 1, :] = jnp.sum(
            cot_ref[a:b, :].astype(F32) * mlp, axis=0, keepdims=True
        )


def middle_back_kernel(
    sizes, mid_ref, cot_ref, grad_ref, attn_ref, mod_ref, out_ref, n_ref, f_ref, sum_ref
):
    count = 2 * sizes[2]
    for a, b, t, s in row_groups(sizes):
        row = t * sizes[2] + s
        unit, inv = normal(mid_ref[a:b, :])
        grad = grad_ref[a:b, :]
        sum_ref[row : row + 1, :] = jnp.sum(grad, axis=0, keepdims=True)
        sum_ref[count + row : count + row + 1, :] = jnp.sum(grad * unit, axis=0, keepdims=True)
        back = normal_back(grad * (1.0 + vec(mod_ref, t, s, 4)), unit, inv)
        total = cot_ref[a:b, :].astype(F32) + back
        out_ref[a:b, :] = total
        put_halves(n_ref, f_ref, a, b, total * vec(mod_ref, t, s, 2))
        sum_ref[2 * count + row : 2 * count + row + 1, :] = jnp.sum(
            total * attn_ref[a:b, :], axis=0, keepdims=True
        )


def first_back_kernel(sizes, x_ref, mid_grad_ref, grad_ref, mod_ref, out_ref, sum_ref):
    count = 2 * sizes[2]
    for a, b, t, s in row_groups(sizes):
        row = t * sizes[2] + s
        unit, inv = normal(x_ref[a:b, :].astype(F32))
        grad = grad_ref[a:b, :]
        sum_ref[row : row + 1, :] = jnp.sum(grad, axis=0, keepdims=True)
        sum_ref[count + row : count + row + 1, :] = jnp.sum(grad * unit, axis=0, keepdims=True)
        back = normal_back(grad * (1.0 + vec(mod_ref, t, s, 1)), unit, inv)
        out_ref[a:b, :] = mid_grad_ref[a:b, :] + back


def call(kernel, outs, *args, flops=1 << 20):
    return pl.pallas_call(
        kernel,
        out_shape=[jax.ShapeDtypeStruct(shape, dtype) for shape, dtype in outs],
        cost_estimate=pl.CostEstimate(flops=flops, bytes_accessed=1 << 20, transcendentals=0),
        compiler_params=pltpu.CompilerParams(vmem_limit_bytes=48 << 20),
    )(*args)


def head_spread(width, head_dim):
    rows = lax.broadcasted_iota(jnp.int32, (width, width), 0) // head_dim
    cols = lax.broadcasted_iota(jnp.int32, (width, width), 1) // head_dim
    return jnp.where(rows == cols, 1.0 / head_dim, 0.0).astype(BF16)


def head_mean(values, spread):
    high = values.astype(BF16)
    low = (values - high.astype(F32)).astype(BF16)
    return dot(high, spread, NN) + dot(low, spread, NN)


def qkv_kernel(sizes, head_dim, near_ref, far_ref, wn_ref, wf_ref, gain_ref, q_ref, kv_ref, raw_ref):
    spread = head_spread(q_ref.shape[1], head_dim)

    def part(c):
        for t in range(2):
            left = stream_rows(near_ref, sizes, t), stream_rows(far_ref, sizes, t)
            total = dot(left[0], wn_ref[t, 0], NN) + dot(left[1], wf_ref[t, 0], NN)
            if c < 2:
                put_stream(raw_ref.at[0], sizes, t, total)
                root = lax.rsqrt(head_mean(total * total, spread) + EPS)
                total = total * root * gain_ref[2 * t + c : 2 * t + c + 1, :]
            put_stream(q_ref if c == 0 else kv_ref.at[0], sizes, t, total)

    for c in range(3):
        pl.when(pl.program_id(0) == c)(functools.partial(part, c))


def qkv_project(near, far, w_near, w_far, gains, sizes, head_dim):
    rows, half = near.shape
    width = gains.shape[1]
    whole = pl.BlockSpec((rows, half), lambda c: (0, 0))
    weight = pl.BlockSpec((2, 1, half, width), lambda c: (0, c, 0, 0))
    return pl.pallas_call(
        functools.partial(qkv_kernel, sizes, head_dim),
        grid=(3,),
        in_specs=[whole, whole, weight, weight, pl.BlockSpec((4, width), lambda c: (0, 0))],
        out_specs=[
            pl.BlockSpec((rows, width), lambda c: (0, 0)),
            pl.BlockSpec((1, rows, width), lambda c: (jnp.maximum(c - 1, 0), 0, 0)),
            pl.BlockSpec((1, rows, width), lambda c: (jnp.minimum(c, 1), 0, 0)),
        ],
        out_shape=[
            jax.ShapeDtypeStruct((rows, width), BF16),
            jax.ShapeDtypeStruct((2, rows, width), BF16),
            jax.ShapeDtypeStruct((2, rows, width), F32),
        ],
        cost_estimate=pl.CostEstimate(flops=1 << 20, bytes_accessed=1 << 20, transcendentals=0),
        compiler_params=pltpu.CompilerParams(vmem_limit_bytes=48 << 20),
    )(
        near,
        far,
        w_near.reshape(2, 3, half, width),
        w_far.reshape(2, 3, half, width),
        gains,
    )


def qkv_back_kernel(
    sizes, head_dim, q_ref, own_ref, c_ref, h_ref, raw_ref, gain_ref, low_ref, sum_ref
):
    width = q_ref.shape[1]
    spread = head_spread(width, head_dim)
    for t in range(2):
        for c in range(2):
            gain = gain_ref[2 * t + c : 2 * t + c + 1, :]
            total = jnp.zeros((1, width), F32)
            for a, b in stream_parts(sizes, t):
                if c == 0:
                    grad = q_ref[a:b, :]
                else:
                    grad = own_ref[0, a:b, :].astype(F32) + c_ref[0, a:b, :].astype(F32)
                    grad = grad + h_ref[0, a:b, :].astype(F32)
                raw = raw_ref[c, a:b, :]
                root = lax.rsqrt(head_mean(raw * raw, spread) + EPS)
                unit = raw * root
                total = total + jnp.sum(grad * unit, axis=0, keepdims=True)
                scaled = grad * gain
                back = root * (scaled - unit * head_mean(scaled * unit, spread))
                low_ref[a:b, c * width : (c + 1) * width] = back.astype(BF16)
            sum_ref[2 * t + c : 2 * t + c + 1, :] = total
        for a, b in stream_parts(sizes, t):
            grad = own_ref[1, a:b, :].astype(F32) + c_ref[1, a:b, :].astype(F32)
            low_ref[a:b, 2 * width :] = (grad + h_ref[1, a:b, :].astype(F32)).astype(BF16)


def mixed_kernel(sizes, near_ref, far_ref, wn_ref, wf_ref, out_ref):
    for t in range(2):
        total = dot(stream_rows(near_ref, sizes, t), wn_ref[t], NN)
        total = total + dot(stream_rows(far_ref, sizes, t), wf_ref[t], NN)
        put_stream(out_ref, sizes, t, total)


GELU_ROOT = 0.7978845608028654
GELU_CUBE = 0.044715


def mlp_kernel(sizes, sn_ref, sf_ref, mn_ref, mf_ref, un_ref, uf_ref, dn_ref, df_ref, h_ref, g_ref):
    for t in range(2):
        pre = dot(stream_rows(sn_ref, sizes, t), un_ref[t], NN)
        pre = pre + dot(stream_rows(sf_ref, sizes, t), uf_ref[t], NN)
        square = pre * pre
        bent = jnp.tanh(GELU_ROOT * pre * (1.0 + GELU_CUBE * square))
        half = 0.5 * (1.0 + bent)
        put_stream(h_ref, sizes, t, pre * half)
        back = dot(stream_rows(mn_ref, sizes, t), dn_ref[t], NN)
        back = back + dot(stream_rows(mf_ref, sizes, t), df_ref[t], NN)
        slope = half + 0.5 * pre * (1.0 - bent * bent) * (
            GELU_ROOT * (1.0 + 3.0 * GELU_CUBE * square)
        )
        put_stream(g_ref, sizes, t, back * slope)


def mlp(second, cot, up, down, sizes):
    rows, half = second[0].shape
    width = up[0].shape[2]
    tile = 384 if width % 384 == 0 else width
    whole = pl.BlockSpec((rows, half), lambda j: (0, 0))
    weight = pl.BlockSpec((2, half, tile), lambda j: (0, 0, j))
    out = pl.BlockSpec((rows, tile), lambda j: (0, j))
    return pl.pallas_call(
        functools.partial(mlp_kernel, sizes),
        grid=(width // tile,),
        in_specs=[whole] * 4 + [weight] * 4,
        out_specs=[out] * 2,
        out_shape=[jax.ShapeDtypeStruct((rows, width), BF16)] * 2,
        cost_estimate=pl.CostEstimate(flops=1 << 20, bytes_accessed=1 << 20, transcendentals=0),
        compiler_params=pltpu.CompilerParams(vmem_limit_bytes=56 << 20),
    )(*second, *cot, *up, *down)


SENT = ((2, 3), (1, 2))
KEPT = ((0, 1), (0, 3))


def project_kernel(sizes, rows_ref, *refs):
    weights, outs = refs[:2], refs[2:]
    per = rows_ref.shape[0] // 4
    for t in range(2):
        left = stream_rows(rows_ref, sizes, t)
        lo, hi = stream_parts(sizes, t)[0]
        for side in range(2):
            chunks = weights[side].shape[0] // 2
            depth = weights[side].shape[2]
            total = dot(left[:, :depth], weights[side][t * chunks], NT)
            for c in range(1, chunks):
                total = total + dot(
                    left[:, c * depth : (c + 1) * depth], weights[side][t * chunks + c], NT
                )
            count = hi - lo
            for k in range(2):
                b = SENT[side][k]
                outs[2 * side][k, lo:hi, :] = total[b * count : (b + 1) * count].astype(BF16)
                b = KEPT[side][k]
                outs[2 * side + 1][k, lo:hi, :] = total[b * count : (b + 1) * count]


def project(rows, near, far, sizes):
    count, depth = rows.shape
    chunks, half, inner = near.shape
    tile = 384 if half % 384 == 0 else half
    weight = pl.BlockSpec((chunks, tile, inner), lambda j: (0, j, 0))
    out = pl.BlockSpec((2, count // 4, tile), lambda j: (0, 0, j))
    shape = (2, count // 4, half)
    return pl.pallas_call(
        functools.partial(project_kernel, sizes),
        grid=(half // tile,),
        in_specs=[pl.BlockSpec((count, depth), lambda j: (0, 0)), weight, weight],
        out_specs=[out] * 4,
        out_shape=[jax.ShapeDtypeStruct(shape, d) for d in (BF16, F32, BF16, F32)],
        cost_estimate=pl.CostEstimate(flops=1 << 20, bytes_accessed=1 << 20, transcendentals=0),
        compiler_params=pltpu.CompilerParams(vmem_limit_bytes=56 << 20),
    )(rows, near, far)


def grad_kernel(sizes, add, left_ref, right_ref, *refs):
    for t in range(2):
        total = dot(stream_rows(left_ref, sizes, t), stream_rows(right_ref, sizes, t), TN)
        if add:
            total = total + refs[0][t].reshape(total.shape).astype(F32)
        refs[-1][t] = total.astype(BF16).reshape(refs[-1].shape[1:])


def stream_grads(left, right, sizes, split, other=None):
    rows, depth = left.shape
    width = right.shape[1]
    tile = 384 if width % 384 == 0 else width
    if split:
        out = pl.BlockSpec((2, 1, depth, tile), lambda j: (0, j, 0, 0))
        shape = (2, width // tile, depth, tile)
    else:
        out = pl.BlockSpec((2, depth, tile), lambda j: (0, 0, j))
        shape = (2, depth, width)
    extra = [] if other is None else [other]
    return pl.pallas_call(
        functools.partial(grad_kernel, sizes, bool(extra)),
        grid=(width // tile,),
        in_specs=[
            pl.BlockSpec((rows, depth), lambda j: (0, 0)),
            pl.BlockSpec((rows, tile), lambda j: (0, j)),
        ]
        + [out] * len(extra),
        out_specs=out,
        out_shape=jax.ShapeDtypeStruct(shape, BF16),
        cost_estimate=pl.CostEstimate(flops=1 << 20, bytes_accessed=1 << 20, transcendentals=0),
        compiler_params=pltpu.CompilerParams(vmem_limit_bytes=48 << 20),
    )(left, right, *extra)


def pair_grad(left, right, sizes, split=False):
    far = trade(stream_grads(left[1], right, sizes, split), "c")
    return stream_grads(left[0], right, sizes, split, far)


def shard_grad(total):
    return lax.psum_scatter(total, ("s", "h"), scatter_dimension=total.ndim - 2, tiled=True)


def own_grad(block):
    return cross(block).astype(F32)


def gather_rows(first, second):
    first_pair = jnp.stack([first, trade(first, "y")])
    second_pair = jnp.stack([second, trade(second, "l")])
    first_far = trade(first_pair, "l")
    second_far = trade(second_pair, "y")
    near = [first_pair[0], first_pair[1], first_far[1], first_far[0]]
    far = [second_pair[0], second_far[0], second_far[1], second_pair[1]]
    return jnp.concatenate(near), jnp.concatenate(far)


def reduce_rows(near_send, near_keep, far_send, far_keep):
    first_in = trade(near_send, "l")
    second_in = trade(far_send, "y")
    first_last = trade((near_keep[1] + first_in[0].astype(F32)).astype(BF16), "y")
    second_last = trade((far_keep[1] + second_in[1].astype(F32)).astype(BF16), "l")
    first = near_keep[0] + first_in[1].astype(F32) + first_last.astype(F32)
    second = far_keep[0] + second_in[0].astype(F32) + second_last.astype(F32)
    return jnp.concatenate([first, second], axis=1), (first_in, second_in)


def sequence_places(seq, sizes):
    img, txt, seqs = sizes
    per = seqs * (img + txt)
    places = [(pl.multiple_of(b * per + seq * img, 16), img) for b in range(4)]
    return places + [(pl.multiple_of(b * per + seqs * img + seq * txt, 16), txt) for b in range(4)]


def sequence_rows(ref, seq, sizes):
    return jnp.concatenate([ref[pl.ds(a, n), :] for a, n in sequence_places(seq, sizes)], axis=0)


def store_rows(ref, seq, sizes, value):
    at = 0
    for a, n in sequence_places(seq, sizes):
        ref[pl.ds(a, n), :] = value[at : at + n]
        at += n


def both_heads(rows, head_dim):
    lane = lax.broadcasted_iota(jnp.int32, rows.shape, 1)
    zero = jnp.zeros_like(rows)
    return jnp.concatenate(
        [jnp.where(lane < head_dim, rows, zero), jnp.where(lane >= head_dim, rows, zero)], axis=0
    )


def join_heads(stacked, head_dim):
    count = stacked.shape[0] // 2
    lane = lax.broadcasted_iota(jnp.int32, (count, stacked.shape[1]), 1)
    return jnp.where(lane < head_dim, stacked[:count], stacked[count:])


def attend_kernel(sizes, head_dim, *refs):
    q_ref, kv_refs = refs[0], refs[1:5]
    bias_ref, out_ref, norm_ref, peak_ref = refs[5:]
    seq = pl.program_id(1)
    query = both_heads(sequence_rows(q_ref, seq, sizes), head_dim)
    keys = jnp.concatenate([sequence_rows(r.at[0], seq, sizes) for r in kv_refs], axis=0)
    values = jnp.concatenate([sequence_rows(r.at[1], seq, sizes) for r in kv_refs], axis=0)
    scores = lax.dot_general(keys, query, NT, preferred_element_type=F32) + bias_ref[0]
    highest = jnp.max(scores, axis=0, keepdims=True)
    weights = jnp.exp(scores - highest)
    total = jnp.sum(weights, axis=0, keepdims=True)
    mixed = lax.dot_general(values, weights.astype(BF16), TN, preferred_element_type=F32)
    mixed = jnp.transpose(mixed * (1.0 / total))
    store_rows(out_ref, seq, sizes, join_heads(mixed, head_dim).astype(BF16))
    norm_ref[0] = highest + jnp.log(total)
    peak_ref[0] = highest


def attend_back_kernel(sizes, head_dim, *refs):
    q_ref, kv_refs = refs[0], refs[1:5]
    bias_ref, norm_ref, grad_ref = refs[5:8]
    gq_ref, gkv_refs = refs[8], refs[9:13]
    seq = pl.program_id(1)
    query = both_heads(sequence_rows(q_ref, seq, sizes), head_dim)
    grad = both_heads(sequence_rows(grad_ref, seq, sizes), head_dim)
    keys = jnp.concatenate([sequence_rows(r.at[0], seq, sizes) for r in kv_refs], axis=0)
    values = jnp.concatenate([sequence_rows(r.at[1], seq, sizes) for r in kv_refs], axis=0)
    scores = lax.dot_general(keys, query, NT, preferred_element_type=F32) + bias_ref[0]
    probs = jnp.exp(scores - norm_ref[0])
    grad_probs = lax.dot_general(values, grad, NT, preferred_element_type=F32)
    inner = jnp.sum(probs * grad_probs, axis=0, keepdims=True)
    grad_scores = (probs * (grad_probs - inner)).astype(BF16)
    grad_values = lax.dot_general(probs.astype(BF16), grad, NN, preferred_element_type=F32)
    grad_keys = lax.dot_general(grad_scores, query, NN, preferred_element_type=F32)
    grad_query = lax.dot_general(keys, grad_scores, TN, preferred_element_type=F32)
    store_rows(gq_ref, seq, sizes, join_heads(jnp.transpose(grad_query), head_dim))
    count = keys.shape[0] // 4
    for j in range(4):
        part = slice(j * count, (j + 1) * count)
        store_rows(gkv_refs[j].at[0], seq, sizes, grad_keys[part].astype(BF16))
        store_rows(gkv_refs[j].at[1], seq, sizes, grad_values[part].astype(BF16))


def attention_specs(rows, keys):
    q_spec = pl.BlockSpec((rows, 128), lambda p, s: (0, p))
    kv_specs = [pl.BlockSpec((2, rows, 128), lambda p, s: (0, 0, p)) for _ in range(4)]
    bias_spec = pl.BlockSpec((1, keys, 1), lambda p, s: (s, 0, 0))
    return q_spec, kv_specs, bias_spec


def attend(queries, key_values, bias, sizes, head_dim):
    rows, width = queries.shape
    seqs, keys = bias.shape[0], bias.shape[1]
    pairs = width // 128
    lanes = 2 * (keys // 4)
    q_spec, kv_specs, bias_spec = attention_specs(rows, keys)
    line = pl.BlockSpec((1, 1, lanes), lambda p, s: (p * seqs + s, 0, 0))
    return pl.pallas_call(
        functools.partial(attend_kernel, sizes, head_dim),
        grid=(pairs, seqs),
        in_specs=[q_spec, *kv_specs, bias_spec],
        out_specs=[q_spec, line, line],
        out_shape=[
            jax.ShapeDtypeStruct((rows, width), BF16),
            jax.ShapeDtypeStruct((pairs * seqs, 1, lanes), F32),
            jax.ShapeDtypeStruct((pairs * seqs, 1, lanes), F32),
        ],
        cost_estimate=pl.CostEstimate(
            flops=pairs * seqs * keys * lanes, bytes_accessed=rows * width, transcendentals=0
        ),
        compiler_params=pltpu.CompilerParams(vmem_limit_bytes=60 << 20),
    )(queries, *key_values, bias)


def attend_back(queries, key_values, bias, norms, grads, sizes, head_dim):
    rows, width = queries.shape
    seqs, keys = bias.shape[0], bias.shape[1]
    pairs = width // 128
    lanes = 2 * (keys // 4)
    q_spec, kv_specs, bias_spec = attention_specs(rows, keys)
    line = pl.BlockSpec((1, 1, lanes), lambda p, s: (p * seqs + s, 0, 0))
    out = pl.pallas_call(
        functools.partial(attend_back_kernel, sizes, head_dim),
        grid=(pairs, seqs),
        in_specs=[q_spec, *kv_specs, bias_spec, line, q_spec],
        out_specs=[q_spec, *kv_specs],
        out_shape=[jax.ShapeDtypeStruct((rows, width), F32)]
        + [jax.ShapeDtypeStruct((2, rows, width), BF16)] * 4,
        cost_estimate=pl.CostEstimate(
            flops=pairs * seqs * keys * lanes, bytes_accessed=rows * width, transcendentals=0
        ),
        compiler_params=pltpu.CompilerParams(vmem_limit_bytes=60 << 20),
    )(queries, *key_values, bias, norms, grads)
    return out[0], out[1:]


def local(
    x_img,
    x_txt,
    cond,
    lengths,
    mod_w,
    qkv_w,
    o_w,
    up_w,
    down_w,
    norm_gain,
    threshold,
    cot_img,
    cot_txt,
):
    shard_count = lax.axis_size("s")
    head_dim = norm_gain.shape[2]
    seqs, img_rows, width = x_img.shape
    txt_real = x_txt.shape[1]
    txt_rows = -(-txt_real // 16) * 16
    sizes = (img_rows, txt_rows, seqs)
    per = seqs * (img_rows + txt_rows)
    feat = mod_w.shape[3]
    block = mod_w.shape[1]
    heads = qkv_w.shape[3] // head_dim
    own = {name: lax.axis_index(name) for name in ("s", "h", "l", "y", "c")}

    source = feature_order(width, shard_count)
    order = one_hot(source)
    count_i = seqs * img_rows

    def arrange(image, text):
        text = jnp.pad(text, ((0, 0), (0, txt_rows - txt_real), (0, 0)))
        both = jnp.concatenate([image.reshape(-1, width), text.reshape(-1, width)], axis=0)
        return jnp.dot(both, order, preferred_element_type=BF16)

    inputs, cot = arrange(x_img, x_txt), arrange(cot_img, cot_txt)

    cond_float = cond.astype(F32)
    cond_act = jax.nn.silu(cond_float).astype(BF16)
    if shard_count == 2:
        cond_all = jnp.concatenate([cond_act, trade(cond_act, "s")], axis=0)
    else:
        cond_all = lax.all_gather(cond_act, "s", axis=0, tiled=True)
    cond_rows = lax.dynamic_index_in_dim(
        cond_all.reshape(cond_all.shape[0], -1, block),
        (own["s"] * 2 + own["h"]) * 2 + own["l"],
        axis=1,
        keepdims=False,
    )
    mod_part = jnp.einsum("sd,tdkf->stkf", cond_rows, mod_w, preferred_element_type=F32)
    if shard_count == 2:
        mod_sum = mod_part[:seqs] + trade(mod_part[seqs:], "s")
    else:
        mod_sum = lax.psum_scatter(mod_part, "s", scatter_dimension=0, tiled=True)
    mod_sum = total_over(mod_sum.reshape(seqs * 12, feat), ("h", "l"))
    mod_full = in_order(in_order(mod_sum, "c", 1), "y", 1)
    modulation = permute_exact(mod_full, order, ((1,), (0,)))

    half = width // 2
    halves = [((per, half), BF16)] * 2
    first_n, first_f, mlp_n, mlp_f = call(
        functools.partial(first_kernel, sizes), halves * 2, inputs, cot, modulation
    )
    first = gather_rows(first_n, first_f)
    cot_rows = gather_rows(mlp_n, mlp_f)
    qkv_near = gather_weight(after(qkv_w.reshape(6, block, -1), mod_sum))
    qkv_far = trade(after(qkv_near, first), "c")
    up_near = gather_weight(after(up_w, first))
    scales = jnp.array([QUERY_SCALE, 1.0], F32)
    gains = jnp.tile(norm_gain * scales[None, :, None], (1, 1, heads)).reshape(4, -1)
    queries, own_kv, raw = qkv_project(*first, qkv_near, qkv_far, gains, sizes, head_dim)
    o_near = gather_weight(after(jnp.swapaxes(o_w, 1, 2), first), own_kv)
    h_kv = trade(own_kv, "h")
    down_near = gather_weight(after(jnp.swapaxes(down_w, 1, 2), own_kv), h_kv)
    o_far = trade(after(o_near, h_kv), "c")
    key_values = [own_kv, trade(own_kv, "c"), h_kv, trade(h_kv, "c")]

    text_bias = []
    for jh, jc in ((0, 0), (0, 1), (1, 0), (1, 1)):
        member = [jnp.zeros((seqs, 4 * img_rows), F32)]
        for jy, jl in ((0, 0), (1, 0), (1, 1), (0, 1)):
            ctx_at = (own["h"] ^ jh) * 2 + (own["l"] ^ jl)
            tp_at = (own["y"] ^ jy) * 2 + (own["c"] ^ jc)
            row = jnp.arange(txt_rows, dtype=jnp.int32)
            slot = (ctx_at * 4 + tp_at) * txt_real + row
            allowed = (row < txt_real)[None, :] & (slot[None, :] < lengths[:, None])
            member.append(jnp.where(allowed, 0.0, MASKED))
        text_bias.append(jnp.concatenate(member, axis=1))
    bias = jnp.concatenate(text_bias, axis=1)[:, :, None]

    attended, log_norm, highest = attend(queries, key_values, bias, sizes, head_dim)
    attn_out, _ = reduce_rows(*project(attended, o_near, o_far, sizes))
    mid, second_n, second_f = call(
        functools.partial(middle_kernel, sizes),
        [((per, width), F32), *halves],
        inputs,
        attn_out,
        modulation,
    )
    second = gather_rows(second_n, second_f)
    up_far = trade(after(up_near, second_n), "c")
    down_far = trade(after(down_near, second), "c")
    hidden, pre_grad = mlp(second, cot_rows, (up_near, up_far), (down_near, down_far), sizes)

    down_far_grad = stream_grads(cot_rows[1], hidden, sizes, False)
    up_far_grad = stream_grads(second[1], after(pre_grad, down_far_grad), sizes, False)
    hidden = after(hidden, up_far_grad)
    down_total = stream_grads(cot_rows[0], hidden, sizes, False, trade(down_far_grad, "c"))
    up_total = stream_grads(second[0], pre_grad, sizes, False, trade(up_far_grad, "c"))
    pre_grad = after(pre_grad, (down_total, up_total))
    second_grad, _ = reduce_rows(*project(pre_grad, up_near, up_far, sizes))
    down_shard, up_shard = shard_grad(down_total), shard_grad(up_total)
    mid_grad, attn_n, attn_f, two_sums = call(
        functools.partial(middle_back_kernel, sizes),
        [((per, width), F32), *halves, ((6 * seqs, width), F32)],
        mid,
        cot,
        second_grad,
        attn_out,
        modulation,
    )
    attn_rows = gather_rows(attn_n, attn_f)
    (mixed_grad,) = call(
        functools.partial(mixed_kernel, sizes),
        [(attended.shape, BF16)],
        *attn_rows,
        o_near,
        o_far,
    )
    mixed_grad = after(mixed_grad, (down_total, up_total))
    query_sum, kv_grads = attend_back(
        queries, key_values, bias, log_norm, mixed_grad, sizes, head_dim
    )
    h_low = (kv_grads[2].astype(F32) + trade(kv_grads[3], "c").astype(F32)).astype(BF16)
    h_grads = trade(h_low, "h")
    c_grads = trade(kv_grads[1], "c")

    mlp_out, _ = reduce_rows(*project(after(hidden, h_low), down_near, down_far, sizes))
    results, gate_sums = call(
        functools.partial(last_kernel, sizes),
        [((per, width), BF16), ((2 * seqs, width), F32)],
        mid,
        mlp_out,
        cot,
        modulation,
    )
    o_total = pair_grad(attn_rows, after(attended, query_sum), sizes)
    grad_down, grad_up = own_grad(down_shard), own_grad(up_shard)
    grad_o = own_grad(shard_grad(after(o_total, up_shard)))

    low_all, gain_sums = call(
        functools.partial(qkv_back_kernel, sizes, head_dim),
        [((4 * per, 3 * heads * head_dim), BF16), (gains.shape, F32)],
        after(query_sum, (mlp_out, o_total)),
        kv_grads[0],
        c_grads,
        h_grads,
        raw,
        gains,
    )
    gain_terms = jnp.sum(gain_sums.reshape(2, 2, heads, head_dim), axis=2) * scales[None, :, None]
    low_all = after(low_all, (grad_down, grad_up, mlp_out))
    grad_qkv = own_grad(shard_grad(pair_grad(first, low_all, sizes, True)))
    first_grad, _ = reduce_rows(*project(low_all, qkv_near, qkv_far, sizes))
    input_grads, one_sums = call(
        functools.partial(first_back_kernel, sizes),
        [((per, width), F32), ((4 * seqs, width), F32)],
        inputs,
        mid_grad,
        first_grad,
        modulation,
    )

    back = ((1,), (1,))

    def restore(moved):
        return (
            moved[:count_i].reshape(seqs, img_rows, width),
            moved[count_i:].reshape(seqs, txt_rows, width)[:, :txt_real],
        )

    out_img, out_txt = restore(
        lax.dot_general(results, order, (back, ((), ())), preferred_element_type=BF16)
    )
    grad_img, grad_txt = restore(permute_exact(input_grads, order, back))

    lanes = highest.shape[2] // 2
    row = jnp.arange(lanes, dtype=jnp.int32)
    valid = (row < 4 * img_rows) | ((row - 4 * img_rows) % txt_rows < txt_real)
    tops = highest.reshape(-1, seqs, 2, lanes)
    tops = jnp.max(jnp.where(valid, tops, -jnp.inf), axis=(1, 3)).reshape(1, heads)
    places = jnp.arange(4 * heads)[None, :] // heads
    tops = jnp.where(places == own["y"] * 2 + own["l"], jnp.tile(tops, (1, 4)), MASKED)

    count = 2 * seqs
    mod_low = jnp.concatenate(
        [one_sums, two_sums[2 * count :], two_sums[: 2 * count], gate_sums], axis=0
    ).astype(BF16)
    mod_count = mod_low.shape[0]
    mod_low = lax.dot_general(mod_low, order, (back, ((), ())), preferred_element_type=F32)
    extra = [gain_terms.reshape(1, -1), tops]
    extra = jnp.concatenate([jnp.pad(e, ((0, 0), (0, feat - e.shape[1]))) for e in extra])
    extra = jnp.pad(extra, ((0, -(mod_count + 2) % 8), (0, 0)))
    mod_low = jnp.concatenate([mod_low, jnp.tile(extra, (1, width // feat))], axis=0)
    is_top = jnp.arange(mod_low.shape[0])[:, None] == mod_count + 1

    def join(first, second):
        return jnp.where(is_top, jnp.maximum(first, second), first + second)

    quarters = [mod_low[:, k * feat : (k + 1) * feat] for k in range(width // feat)]
    at_c, at_y = own["c"] == 0, own["y"] == 0
    keep = [jnp.where(at_c, quarters[2 * k], quarters[2 * k + 1]) for k in range(2)]
    send = [jnp.where(at_c, quarters[2 * k + 1], quarters[2 * k]) for k in range(2)]
    pair = join(jnp.stack(keep), trade(jnp.stack(send), "c"))
    mod_sum = join(
        jnp.where(at_y, pair[0], pair[1]), trade(jnp.where(at_y, pair[1], pair[0]), "y")
    )
    for axis in ("l", "h"):
        mod_sum = join(mod_sum, trade(mod_sum, axis))
    if shard_count == 2:
        mod_members = jnp.stack([mod_sum, trade(mod_sum, "s")])
    else:
        mod_members = lax.all_gather(mod_sum, "s")
    gain_grad = jnp.sum(mod_members[:, mod_count], axis=0)[: 4 * head_dim]
    gain_grad = gain_grad.reshape(norm_gain.shape)
    tops = jnp.max(mod_members[:, mod_count + 1], axis=0)[: 4 * heads]
    peaks = lax.dynamic_slice_in_dim(tops, (own["y"] * 2 + own["c"]) * heads, heads)
    mod_seqs = mod_members[:, :mod_count].astype(BF16).reshape(-1, 6, 2, seqs, feat)
    mod_seqs = mod_seqs.transpose(2, 0, 3, 1, 4).reshape(2, -1, 6, feat)
    grad_mod = jnp.einsum("sd,tskf->tdkf", cond_rows, mod_seqs, preferred_element_type=F32)
    cond_part = jnp.einsum("tskf,tdkf->sd", mod_seqs, mod_w, preferred_element_type=F32)
    cond_part = in_order(in_order(total_over(cond_part, ("c", "y")), "l", 1), "h", 1)
    if shard_count == 2:
        mine, other = cond_part[:seqs], trade(cond_part[seqs:], "s")
        at_s = own["s"] == 0
        cond_total = jnp.concatenate(
            [jnp.where(at_s, mine, other), jnp.where(at_s, other, mine)], axis=1
        )
    else:
        cond_cols = lax.all_gather(cond_part, "s", axis=1, tiled=True)
        cond_total = lax.dynamic_slice_in_dim(cond_cols, own["s"] * seqs, seqs, axis=0)
    unused, silu_vjp = jax.vjp(jax.nn.silu, cond_float)
    grad_cond = silu_vjp(cond_total)[0]

    factor = jnp.sqrt(threshold / jnp.maximum(peaks, threshold))
    columns = jnp.repeat(factor, head_dim)
    clipped = qkv_w[:, :2].astype(F32) * columns
    return (
        out_img,
        out_txt,
        grad_img,
        grad_txt,
        grad_cond,
        grad_mod,
        grad_qkv,
        jnp.swapaxes(grad_o, 1, 2),
        grad_up,
        jnp.swapaxes(grad_down, 1, 2),
        gain_grad,
        clipped,
        peaks,
    )


def solution(mesh):
    shard, ctx, tp = (mesh.shape[name] for name in ("shard", "ctx", "tp"))
    fine = Mesh(mesh.devices.reshape(shard, ctx // 2, 2, tp // 2, 2), ("s", "h", "l", "y", "c"))
    ctx_axes, tp_axes = ("h", "l"), ("y", "c")
    rows = P("s", ctx_axes + tp_axes, None)
    weight = ("s",) + ctx_axes
    mod = P(None, weight, None, tp_axes)
    qkv = P(None, None, weight, tp_axes)
    inward = P(None, tp_axes, weight)
    outward = P(None, weight, tp_axes)
    return jax.shard_map(
        local,
        mesh=fine,
        in_specs=(
            rows,
            rows,
            P("s", None),
            P("s"),
            mod,
            qkv,
            inward,
            outward,
            inward,
            P(),
            P(),
            rows,
            rows,
        ),
        out_specs=(
            rows,
            rows,
            rows,
            rows,
            P("s", None),
            mod,
            qkv,
            inward,
            outward,
            inward,
            P(),
            qkv,
            P(tp_axes),
        ),
        check_vma=False,
    )
```

```python
import functools

import jax
import jax.numpy as jnp
from jax import lax
from jax.experimental import pallas as pl
from jax.experimental.pallas import tpu as pltpu
from jax.sharding import Mesh, PartitionSpec as P

EPS = 1e-06
QUERY_SCALE = 0.125
BF16 = jnp.bfloat16
F32 = jnp.float32
MASKED = -1e30
NT = (((1,), (1,)), ((), ()))
TN = (((0,), (0,)), ((), ()))
NN = (((1,), (0,)), ((), ()))


def trade(values, axis):
    return lax.ppermute(values, axis, [(0, 1), (1, 0)])


def cross(values):
    moved = lax.ppermute(values, ("l", "c"), [(1, 2), (2, 1)])
    return jnp.where(lax.axis_index("l") == lax.axis_index("c"), values, moved)


def in_order(values, axis, dim):
    other = trade(values, axis)
    first = lax.axis_index(axis) == 0
    return jnp.concatenate(
        [jnp.where(first, values, other), jnp.where(first, other, values)], axis=dim
    )


def total_over(values, axes):
    for axis in axes:
        values = values + trade(values, axis)
    return values


def highest_over(values, axes):
    for axis in axes:
        values = jnp.maximum(values, trade(values, axis))
    return values


def after(values, others):
    return lax.optimization_barrier((values, others))[0]


def feature_order(width, shard_count):
    place = jnp.arange(width, dtype=jnp.int32)
    block = width // (shard_count * 4)
    member = place // block
    low = member // (shard_count * 2) ^ lax.axis_index("c")
    return (member % (shard_count * 2) * 2 + low) * block + place % block


def one_hot(source):
    width = source.shape[0]
    rows = lax.broadcasted_iota(jnp.int32, (width, width), 0)
    return (rows == source[None, :]).astype(BF16)


def permute_exact(values, matrix, dims):
    high = lax.reduce_precision(values, 8, 7)
    rest = values - high
    middle = lax.reduce_precision(rest, 8, 7)
    low = rest - middle
    parts = [
        lax.dot_general(part.astype(BF16), matrix, (dims, ((), ())), preferred_element_type=F32)
        for part in (high, middle, low)
    ]
    return parts[0] + (parts[1] + parts[2])


def gather_weight(shard, others=None):
    own = cross(shard)
    if others is not None:
        own = after(own, others)
    return lax.all_gather(own, ("s", "h"), axis=1, tiled=True)


def dot(left, right, dims):
    return lax.dot_general(left, right, dims, preferred_element_type=F32)


def row_groups(sizes):
    img, txt, seqs = sizes
    base = seqs * img
    groups = [(s * img, (s + 1) * img, 0, s) for s in range(seqs)]
    return groups + [(base + s * txt, base + (s + 1) * txt, 1, s) for s in range(seqs)]


def stream_parts(sizes, stream):
    img, txt, seqs = sizes
    per = seqs * (img + txt)
    lo, hi = ((0, seqs * img), (seqs * img, per))[stream]
    return [(b * per + lo, b * per + hi) for b in range(4)]


def stream_rows(ref, sizes, stream):
    return jnp.concatenate([ref[a:b, :] for a, b in stream_parts(sizes, stream)], axis=0)


def put_stream(ref, sizes, stream, value):
    at = 0
    for a, b in stream_parts(sizes, stream):
        ref[a:b, :] = value[at : at + b - a].astype(ref.dtype)
        at += b - a


def vec(ref, stream, seq, k):
    row = (seq * 2 + stream) * 6 + k
    return ref[row : row + 1, :]


def normal(values):
    center = values - jnp.mean(values, axis=-1, keepdims=True)
    inv = lax.rsqrt(jnp.mean(center * center, axis=-1, keepdims=True) + EPS)
    return center * inv, inv


def normal_back(grad, unit, inv):
    mean = jnp.mean(grad, axis=-1, keepdims=True)
    return inv * (grad - mean - unit * jnp.mean(grad * unit, axis=-1, keepdims=True))


def put_halves(near_ref, far_ref, a, b, value):
    half = value.shape[1] // 2
    near_ref[a:b, :] = value[:, :half].astype(near_ref.dtype)
    far_ref[a:b, :] = value[:, half:].astype(far_ref.dtype)


def first_kernel(sizes, x_ref, cot_ref, mod_ref, n1_ref, f1_ref, n2_ref, f2_ref):
    for a, b, t, s in row_groups(sizes):
        unit, _ = normal(x_ref[a:b, :].astype(F32))
        put_halves(n1_ref, f1_ref, a, b, unit * (1.0 + vec(mod_ref, t, s, 1)) + vec(mod_ref, t, s, 0))
        put_halves(n2_ref, f2_ref, a, b, cot_ref[a:b, :].astype(F32) * vec(mod_ref, t, s, 5))


def middle_kernel(sizes, x_ref, attn_ref, mod_ref, mid_ref, n_ref, f_ref):
    for a, b, t, s in row_groups(sizes):
        mid = x_ref[a:b, :].astype(F32) + vec(mod_ref, t, s, 2) * attn_ref[a:b, :]
        mid_ref[a:b, :] = mid
        unit, _ = normal(mid)
        put_halves(n_ref, f_ref, a, b, unit * (1.0 + vec(mod_ref, t, s, 4)) + vec(mod_ref, t, s, 3))


def last_kernel(sizes, mid_ref, mlp_ref, cot_ref, mod_ref, out_ref, sum_ref):
    for a, b, t, s in row_groups(sizes):
        mlp = mlp_ref[a:b, :]
        out_ref[a:b, :] = (mid_ref[a:b, :] + vec(mod_ref, t, s, 5) * mlp).astype(BF16)
        row = t * sizes[2] + s
        sum_ref[row : row + 1, :] = jnp.sum(
            cot_ref[a:b, :].astype(F32) * mlp, axis=0, keepdims=True
        )


def middle_back_kernel(
    sizes, mid_ref, cot_ref, grad_ref, attn_ref, mod_ref, out_ref, n_ref, f_ref, sum_ref
):
    count = 2 * sizes[2]
    for a, b, t, s in row_groups(sizes):
        row = t * sizes[2] + s
        unit, inv = normal(mid_ref[a:b, :])
        grad = grad_ref[a:b, :]
        sum_ref[row : row + 1, :] = jnp.sum(grad, axis=0, keepdims=True)
        sum_ref[count + row : count + row + 1, :] = jnp.sum(grad * unit, axis=0, keepdims=True)
        back = normal_back(grad * (1.0 + vec(mod_ref, t, s, 4)), unit, inv)
        total = cot_ref[a:b, :].astype(F32) + back
        out_ref[a:b, :] = total
        put_halves(n_ref, f_ref, a, b, total * vec(mod_ref, t, s, 2))
        sum_ref[2 * count + row : 2 * count + row + 1, :] = jnp.sum(
            total * attn_ref[a:b, :], axis=0, keepdims=True
        )


def first_back_kernel(sizes, x_ref, mid_grad_ref, grad_ref, mod_ref, out_ref, sum_ref):
    count = 2 * sizes[2]
    for a, b, t, s in row_groups(sizes):
        row = t * sizes[2] + s
        unit, inv = normal(x_ref[a:b, :].astype(F32))
        grad = grad_ref[a:b, :]
        sum_ref[row : row + 1, :] = jnp.sum(grad, axis=0, keepdims=True)
        sum_ref[count + row : count + row + 1, :] = jnp.sum(grad * unit, axis=0, keepdims=True)
        back = normal_back(grad * (1.0 + vec(mod_ref, t, s, 1)), unit, inv)
        out_ref[a:b, :] = mid_grad_ref[a:b, :] + back


def call(kernel, outs, *args, flops=1 << 20):
    return pl.pallas_call(
        kernel,
        out_shape=[jax.ShapeDtypeStruct(shape, dtype) for shape, dtype in outs],
        cost_estimate=pl.CostEstimate(flops=flops, bytes_accessed=1 << 20, transcendentals=0),
        compiler_params=pltpu.CompilerParams(vmem_limit_bytes=48 << 20),
    )(*args)


def head_spread(width, head_dim):
    rows = lax.broadcasted_iota(jnp.int32, (width, width), 0) // head_dim
    cols = lax.broadcasted_iota(jnp.int32, (width, width), 1) // head_dim
    return jnp.where(rows == cols, 1.0 / head_dim, 0.0).astype(BF16)


def head_mean(values, spread):
    high = values.astype(BF16)
    low = (values - high.astype(F32)).astype(BF16)
    return dot(high, spread, NN) + dot(low, spread, NN)


def qkv_kernel(sizes, head_dim, near_ref, far_ref, wn_ref, wf_ref, gain_ref, q_ref, kv_ref, raw_ref):
    spread = head_spread(q_ref.shape[1], head_dim)

    def part(c):
        for t in range(2):
            left = stream_rows(near_ref, sizes, t), stream_rows(far_ref, sizes, t)
            total = dot(left[0], wn_ref[t, 0], NN) + dot(left[1], wf_ref[t, 0], NN)
            if c < 2:
                put_stream(raw_ref.at[0], sizes, t, total)
                root = lax.rsqrt(head_mean(total * total, spread) + EPS)
                total = total * root * gain_ref[2 * t + c : 2 * t + c + 1, :]
            put_stream(q_ref if c == 0 else kv_ref.at[0], sizes, t, total)

    for c in range(3):
        pl.when(pl.program_id(0) == c)(functools.partial(part, c))


def qkv_project(near, far, w_near, w_far, gains, sizes, head_dim):
    rows, half = near.shape
    width = gains.shape[1]
    whole = pl.BlockSpec((rows, half), lambda c: (0, 0))
    weight = pl.BlockSpec((2, 1, half, width), lambda c: (0, c, 0, 0))
    return pl.pallas_call(
        functools.partial(qkv_kernel, sizes, head_dim),
        grid=(3,),
        in_specs=[whole, whole, weight, weight, pl.BlockSpec((4, width), lambda c: (0, 0))],
        out_specs=[
            pl.BlockSpec((rows, width), lambda c: (0, 0)),
            pl.BlockSpec((1, rows, width), lambda c: (jnp.maximum(c - 1, 0), 0, 0)),
            pl.BlockSpec((1, rows, width), lambda c: (jnp.minimum(c, 1), 0, 0)),
        ],
        out_shape=[
            jax.ShapeDtypeStruct((rows, width), BF16),
            jax.ShapeDtypeStruct((2, rows, width), BF16),
            jax.ShapeDtypeStruct((2, rows, width), F32),
        ],
        cost_estimate=pl.CostEstimate(flops=1 << 20, bytes_accessed=1 << 20, transcendentals=0),
        compiler_params=pltpu.CompilerParams(vmem_limit_bytes=48 << 20),
    )(
        near,
        far,
        w_near.reshape(2, 3, half, width),
        w_far.reshape(2, 3, half, width),
        gains,
    )


def qkv_back_kernel(
    sizes, head_dim, q_ref, own_ref, c_ref, h_ref, raw_ref, gain_ref, low_ref, sum_ref
):
    width = q_ref.shape[1]
    spread = head_spread(width, head_dim)
    for t in range(2):
        for c in range(2):
            gain = gain_ref[2 * t + c : 2 * t + c + 1, :]
            total = jnp.zeros((1, width), F32)
            for a, b in stream_parts(sizes, t):
                if c == 0:
                    grad = q_ref[a:b, :]
                else:
                    grad = own_ref[0, a:b, :].astype(F32) + c_ref[0, a:b, :].astype(F32)
                    grad = grad + h_ref[0, a:b, :].astype(F32)
                raw = raw_ref[c, a:b, :]
                root = lax.rsqrt(head_mean(raw * raw, spread) + EPS)
                unit = raw * root
                total = total + jnp.sum(grad * unit, axis=0, keepdims=True)
                scaled = grad * gain
                back = root * (scaled - unit * head_mean(scaled * unit, spread))
                low_ref[a:b, c * width : (c + 1) * width] = back.astype(BF16)
            sum_ref[2 * t + c : 2 * t + c + 1, :] = total
        for a, b in stream_parts(sizes, t):
            grad = own_ref[1, a:b, :].astype(F32) + c_ref[1, a:b, :].astype(F32)
            low_ref[a:b, 2 * width :] = (grad + h_ref[1, a:b, :].astype(F32)).astype(BF16)


def mixed_kernel(sizes, near_ref, far_ref, wn_ref, wf_ref, out_ref):
    for t in range(2):
        total = dot(stream_rows(near_ref, sizes, t), wn_ref[t], NN)
        total = total + dot(stream_rows(far_ref, sizes, t), wf_ref[t], NN)
        put_stream(out_ref, sizes, t, total)


GELU_ROOT = 0.7978845608028654
GELU_CUBE = 0.044715


def mlp_kernel(sizes, sn_ref, sf_ref, mn_ref, mf_ref, un_ref, uf_ref, dn_ref, df_ref, h_ref, g_ref):
    for t in range(2):
        pre = dot(stream_rows(sn_ref, sizes, t), un_ref[t], NN)
        pre = pre + dot(stream_rows(sf_ref, sizes, t), uf_ref[t], NN)
        square = pre * pre
        bent = jnp.tanh(GELU_ROOT * pre * (1.0 + GELU_CUBE * square))
        half = 0.5 * (1.0 + bent)
        put_stream(h_ref, sizes, t, pre * half)
        back = dot(stream_rows(mn_ref, sizes, t), dn_ref[t], NN)
        back = back + dot(stream_rows(mf_ref, sizes, t), df_ref[t], NN)
        slope = half + 0.5 * pre * (1.0 - bent * bent) * (
            GELU_ROOT * (1.0 + 3.0 * GELU_CUBE * square)
        )
        put_stream(g_ref, sizes, t, back * slope)


def mlp(second, cot, up, down, sizes):
    rows, half = second[0].shape
    width = up[0].shape[2]
    tile = 384 if width % 384 == 0 else width
    whole = pl.BlockSpec((rows, half), lambda j: (0, 0))
    weight = pl.BlockSpec((2, half, tile), lambda j: (0, 0, j))
    out = pl.BlockSpec((rows, tile), lambda j: (0, j))
    return pl.pallas_call(
        functools.partial(mlp_kernel, sizes),
        grid=(width // tile,),
        in_specs=[whole] * 4 + [weight] * 4,
        out_specs=[out] * 2,
        out_shape=[jax.ShapeDtypeStruct((rows, width), BF16)] * 2,
        cost_estimate=pl.CostEstimate(flops=1 << 20, bytes_accessed=1 << 20, transcendentals=0),
        compiler_params=pltpu.CompilerParams(vmem_limit_bytes=56 << 20),
    )(*second, *cot, *up, *down)


SENT = ((2, 3), (1, 2))
KEPT = ((0, 1), (0, 3))


def project_kernel(sizes, rows_ref, *refs):
    weights, outs = refs[:2], refs[2:]
    per = rows_ref.shape[0] // 4
    for t in range(2):
        left = stream_rows(rows_ref, sizes, t)
        lo, hi = stream_parts(sizes, t)[0]
        for side in range(2):
            chunks = weights[side].shape[0] // 2
            depth = weights[side].shape[2]
            total = dot(left[:, :depth], weights[side][t * chunks], NT)
            for c in range(1, chunks):
                total = total + dot(
                    left[:, c * depth : (c + 1) * depth], weights[side][t * chunks + c], NT
                )
            count = hi - lo
            for k in range(2):
                b = SENT[side][k]
                outs[2 * side][k, lo:hi, :] = total[b * count : (b + 1) * count].astype(BF16)
                b = KEPT[side][k]
                outs[2 * side + 1][k, lo:hi, :] = total[b * count : (b + 1) * count]


def project(rows, near, far, sizes):
    count, depth = rows.shape
    chunks, half, inner = near.shape
    tile = 384 if half % 384 == 0 else half
    weight = pl.BlockSpec((chunks, tile, inner), lambda j: (0, j, 0))
    out = pl.BlockSpec((2, count // 4, tile), lambda j: (0, 0, j))
    shape = (2, count // 4, half)
    return pl.pallas_call(
        functools.partial(project_kernel, sizes),
        grid=(half // tile,),
        in_specs=[pl.BlockSpec((count, depth), lambda j: (0, 0)), weight, weight],
        out_specs=[out] * 4,
        out_shape=[jax.ShapeDtypeStruct(shape, d) for d in (BF16, F32, BF16, F32)],
        cost_estimate=pl.CostEstimate(flops=1 << 20, bytes_accessed=1 << 20, transcendentals=0),
        compiler_params=pltpu.CompilerParams(vmem_limit_bytes=56 << 20),
    )(rows, near, far)


def grad_kernel(sizes, add, left_ref, right_ref, *refs):
    for t in range(2):
        total = dot(stream_rows(left_ref, sizes, t), stream_rows(right_ref, sizes, t), TN)
        if add:
            total = total + refs[0][t].reshape(total.shape).astype(F32)
        refs[-1][t] = total.astype(BF16).reshape(refs[-1].shape[1:])


def stream_grads(left, right, sizes, split, other=None):
    rows, depth = left.shape
    width = right.shape[1]
    tile = 384 if width % 384 == 0 else width
    if split:
        out = pl.BlockSpec((2, 1, depth, tile), lambda j: (0, j, 0, 0))
        shape = (2, width // tile, depth, tile)
    else:
        out = pl.BlockSpec((2, depth, tile), lambda j: (0, 0, j))
        shape = (2, depth, width)
    extra = [] if other is None else [other]
    return pl.pallas_call(
        functools.partial(grad_kernel, sizes, bool(extra)),
        grid=(width // tile,),
        in_specs=[
            pl.BlockSpec((rows, depth), lambda j: (0, 0)),
            pl.BlockSpec((rows, tile), lambda j: (0, j)),
        ]
        + [out] * len(extra),
        out_specs=out,
        out_shape=jax.ShapeDtypeStruct(shape, BF16),
        cost_estimate=pl.CostEstimate(flops=1 << 20, bytes_accessed=1 << 20, transcendentals=0),
        compiler_params=pltpu.CompilerParams(vmem_limit_bytes=48 << 20),
    )(left, right, *extra)


def pair_grad(left, right, sizes, split=False):
    far = trade(stream_grads(left[1], right, sizes, split), "c")
    return stream_grads(left[0], right, sizes, split, far)


def shard_grad(total):
    return lax.psum_scatter(total, ("s", "h"), scatter_dimension=total.ndim - 2, tiled=True)


def own_grad(block):
    return cross(block).astype(F32)


def gather_rows(first, second):
    first_pair = jnp.stack([first, trade(first, "y")])
    second_pair = jnp.stack([second, trade(second, "l")])
    first_far = trade(first_pair, "l")
    second_far = trade(second_pair, "y")
    near = [first_pair[0], first_pair[1], first_far[1], first_far[0]]
    far = [second_pair[0], second_far[0], second_far[1], second_pair[1]]
    return jnp.concatenate(near), jnp.concatenate(far)


def reduce_rows(near_send, near_keep, far_send, far_keep):
    first_in = trade(near_send, "l")
    second_in = trade(far_send, "y")
    first_last = trade((near_keep[1] + first_in[0].astype(F32)).astype(BF16), "y")
    second_last = trade((far_keep[1] + second_in[1].astype(F32)).astype(BF16), "l")
    first = near_keep[0] + first_in[1].astype(F32) + first_last.astype(F32)
    second = far_keep[0] + second_in[0].astype(F32) + second_last.astype(F32)
    return jnp.concatenate([first, second], axis=1), (first_in, second_in)


def sequence_places(seq, sizes):
    img, txt, seqs = sizes
    per = seqs * (img + txt)
    places = [(pl.multiple_of(b * per + seq * img, 16), img) for b in range(4)]
    return places + [(pl.multiple_of(b * per + seqs * img + seq * txt, 16), txt) for b in range(4)]


def sequence_rows(ref, seq, sizes):
    return jnp.concatenate([ref[pl.ds(a, n), :] for a, n in sequence_places(seq, sizes)], axis=0)


def store_rows(ref, seq, sizes, value):
    at = 0
    for a, n in sequence_places(seq, sizes):
        ref[pl.ds(a, n), :] = value[at : at + n]
        at += n


def both_heads(rows, head_dim):
    lane = lax.broadcasted_iota(jnp.int32, rows.shape, 1)
    zero = jnp.zeros_like(rows)
    return jnp.concatenate(
        [jnp.where(lane < head_dim, rows, zero), jnp.where(lane >= head_dim, rows, zero)], axis=0
    )


def join_heads(stacked, head_dim):
    count = stacked.shape[0] // 2
    lane = lax.broadcasted_iota(jnp.int32, (count, stacked.shape[1]), 1)
    return jnp.where(lane < head_dim, stacked[:count], stacked[count:])


def attend_kernel(sizes, head_dim, *refs):
    q_ref, kv_refs = refs[0], refs[1:5]
    bias_ref, out_ref, norm_ref, peak_ref = refs[5:]
    seq = pl.program_id(1)
    query = both_heads(sequence_rows(q_ref, seq, sizes), head_dim)
    keys = jnp.concatenate([sequence_rows(r.at[0], seq, sizes) for r in kv_refs], axis=0)
    values = jnp.concatenate([sequence_rows(r.at[1], seq, sizes) for r in kv_refs], axis=0)
    scores = lax.dot_general(keys, query, NT, preferred_element_type=F32) + bias_ref[0]
    highest = jnp.max(scores, axis=0, keepdims=True)
    weights = jnp.exp(scores - highest)
    total = jnp.sum(weights, axis=0, keepdims=True)
    mixed = lax.dot_general(values, weights.astype(BF16), TN, preferred_element_type=F32)
    mixed = jnp.transpose(mixed * (1.0 / total))
    store_rows(out_ref, seq, sizes, join_heads(mixed, head_dim).astype(BF16))
    norm_ref[0] = highest + jnp.log(total)
    peak_ref[0] = highest


def attend_back_kernel(sizes, head_dim, *refs):
    q_ref, kv_refs = refs[0], refs[1:5]
    bias_ref, norm_ref, grad_ref = refs[5:8]
    gq_ref, gkv_refs = refs[8], refs[9:13]
    seq = pl.program_id(1)
    query = both_heads(sequence_rows(q_ref, seq, sizes), head_dim)
    grad = both_heads(sequence_rows(grad_ref, seq, sizes), head_dim)
    keys = jnp.concatenate([sequence_rows(r.at[0], seq, sizes) for r in kv_refs], axis=0)
    values = jnp.concatenate([sequence_rows(r.at[1], seq, sizes) for r in kv_refs], axis=0)
    scores = lax.dot_general(keys, query, NT, preferred_element_type=F32) + bias_ref[0]
    probs = jnp.exp(scores - norm_ref[0])
    grad_probs = lax.dot_general(values, grad, NT, preferred_element_type=F32)
    inner = jnp.sum(probs * grad_probs, axis=0, keepdims=True)
    grad_scores = (probs * (grad_probs - inner)).astype(BF16)
    grad_values = lax.dot_general(probs.astype(BF16), grad, NN, preferred_element_type=F32)
    grad_keys = lax.dot_general(grad_scores, query, NN, preferred_element_type=F32)
    grad_query = lax.dot_general(keys, grad_scores, TN, preferred_element_type=F32)
    store_rows(gq_ref, seq, sizes, join_heads(jnp.transpose(grad_query), head_dim))
    count = keys.shape[0] // 4
    for j in range(4):
        part = slice(j * count, (j + 1) * count)
        store_rows(gkv_refs[j].at[0], seq, sizes, grad_keys[part].astype(BF16))
        store_rows(gkv_refs[j].at[1], seq, sizes, grad_values[part].astype(BF16))


def attention_specs(rows, keys):
    q_spec = pl.BlockSpec((rows, 128), lambda p, s: (0, p))
    kv_specs = [pl.BlockSpec((2, rows, 128), lambda p, s: (0, 0, p)) for _ in range(4)]
    bias_spec = pl.BlockSpec((1, keys, 1), lambda p, s: (s, 0, 0))
    return q_spec, kv_specs, bias_spec


def attend(queries, key_values, bias, sizes, head_dim):
    rows, width = queries.shape
    seqs, keys = bias.shape[0], bias.shape[1]
    pairs = width // 128
    lanes = 2 * (keys // 4)
    q_spec, kv_specs, bias_spec = attention_specs(rows, keys)
    line = pl.BlockSpec((1, 1, lanes), lambda p, s: (p * seqs + s, 0, 0))
    return pl.pallas_call(
        functools.partial(attend_kernel, sizes, head_dim),
        grid=(pairs, seqs),
        in_specs=[q_spec, *kv_specs, bias_spec],
        out_specs=[q_spec, line, line],
        out_shape=[
            jax.ShapeDtypeStruct((rows, width), BF16),
            jax.ShapeDtypeStruct((pairs * seqs, 1, lanes), F32),
            jax.ShapeDtypeStruct((pairs * seqs, 1, lanes), F32),
        ],
        cost_estimate=pl.CostEstimate(
            flops=pairs * seqs * keys * lanes, bytes_accessed=rows * width, transcendentals=0
        ),
        compiler_params=pltpu.CompilerParams(vmem_limit_bytes=60 << 20),
    )(queries, *key_values, bias)


def attend_back(queries, key_values, bias, norms, grads, sizes, head_dim):
    rows, width = queries.shape
    seqs, keys = bias.shape[0], bias.shape[1]
    pairs = width // 128
    lanes = 2 * (keys // 4)
    q_spec, kv_specs, bias_spec = attention_specs(rows, keys)
    line = pl.BlockSpec((1, 1, lanes), lambda p, s: (p * seqs + s, 0, 0))
    out = pl.pallas_call(
        functools.partial(attend_back_kernel, sizes, head_dim),
        grid=(pairs, seqs),
        in_specs=[q_spec, *kv_specs, bias_spec, line, q_spec],
        out_specs=[q_spec, *kv_specs],
        out_shape=[jax.ShapeDtypeStruct((rows, width), F32)]
        + [jax.ShapeDtypeStruct((2, rows, width), BF16)] * 4,
        cost_estimate=pl.CostEstimate(
            flops=pairs * seqs * keys * lanes, bytes_accessed=rows * width, transcendentals=0
        ),
        compiler_params=pltpu.CompilerParams(vmem_limit_bytes=60 << 20),
    )(queries, *key_values, bias, norms, grads)
    return out[0], out[1:]


def local(
    x_img,
    x_txt,
    cond,
    lengths,
    mod_w,
    qkv_w,
    o_w,
    up_w,
    down_w,
    norm_gain,
    threshold,
    cot_img,
    cot_txt,
):
    shard_count = lax.axis_size("s")
    head_dim = norm_gain.shape[2]
    seqs, img_rows, width = x_img.shape
    txt_real = x_txt.shape[1]
    txt_rows = -(-txt_real // 16) * 16
    sizes = (img_rows, txt_rows, seqs)
    per = seqs * (img_rows + txt_rows)
    feat = mod_w.shape[3]
    block = mod_w.shape[1]
    heads = qkv_w.shape[3] // head_dim
    own = {name: lax.axis_index(name) for name in ("s", "h", "l", "y", "c")}

    source = feature_order(width, shard_count)
    order = one_hot(source)
    count_i = seqs * img_rows

    def arrange(image, text):
        text = jnp.pad(text, ((0, 0), (0, txt_rows - txt_real), (0, 0)))
        both = jnp.concatenate([image.reshape(-1, width), text.reshape(-1, width)], axis=0)
        return jnp.dot(both, order, preferred_element_type=BF16)

    inputs, cot = arrange(x_img, x_txt), arrange(cot_img, cot_txt)

    cond_float = cond.astype(F32)
    cond_act = jax.nn.silu(cond_float).astype(BF16)
    if shard_count == 2:
        cond_all = jnp.concatenate([cond_act, trade(cond_act, "s")], axis=0)
    else:
        cond_all = lax.all_gather(cond_act, "s", axis=0, tiled=True)
    cond_rows = lax.dynamic_index_in_dim(
        cond_all.reshape(cond_all.shape[0], -1, block),
        (own["s"] * 2 + own["h"]) * 2 + own["l"],
        axis=1,
        keepdims=False,
    )
    mod_part = jnp.einsum("sd,tdkf->stkf", cond_rows, mod_w, preferred_element_type=F32)
    if shard_count == 2:
        mod_sum = mod_part[:seqs] + trade(mod_part[seqs:], "s")
    else:
        mod_sum = lax.psum_scatter(mod_part, "s", scatter_dimension=0, tiled=True)
    mod_sum = total_over(mod_sum.reshape(seqs * 12, feat), ("h", "l"))
    mod_full = in_order(in_order(mod_sum, "c", 1), "y", 1)
    modulation = permute_exact(mod_full, order, ((1,), (0,)))

    half = width // 2
    halves = [((per, half), BF16)] * 2
    first_n, first_f, mlp_n, mlp_f = call(
        functools.partial(first_kernel, sizes), halves * 2, inputs, cot, modulation
    )
    first = gather_rows(first_n, first_f)
    cot_rows = gather_rows(mlp_n, mlp_f)
    qkv_near = gather_weight(after(qkv_w.reshape(6, block, -1), mod_sum))
    qkv_far = trade(after(qkv_near, first), "c")
    up_near = gather_weight(after(up_w, first))
    scales = jnp.array([QUERY_SCALE, 1.0], F32)
    gains = jnp.tile(norm_gain * scales[None, :, None], (1, 1, heads)).reshape(4, -1)
    queries, own_kv, raw = qkv_project(*first, qkv_near, qkv_far, gains, sizes, head_dim)
    o_near = gather_weight(after(jnp.swapaxes(o_w, 1, 2), first), own_kv)
    h_kv = trade(own_kv, "h")
    down_near = gather_weight(after(jnp.swapaxes(down_w, 1, 2), own_kv), h_kv)
    o_far = trade(after(o_near, h_kv), "c")
    key_values = [own_kv, trade(own_kv, "c"), h_kv, trade(h_kv, "c")]

    text_bias = []
    for jh, jc in ((0, 0), (0, 1), (1, 0), (1, 1)):
        member = [jnp.zeros((seqs, 4 * img_rows), F32)]
        for jy, jl in ((0, 0), (1, 0), (1, 1), (0, 1)):
            ctx_at = (own["h"] ^ jh) * 2 + (own["l"] ^ jl)
            tp_at = (own["y"] ^ jy) * 2 + (own["c"] ^ jc)
            row = jnp.arange(txt_rows, dtype=jnp.int32)
            slot = (ctx_at * 4 + tp_at) * txt_real + row
            allowed = (row < txt_real)[None, :] & (slot[None, :] < lengths[:, None])
            member.append(jnp.where(allowed, 0.0, MASKED))
        text_bias.append(jnp.concatenate(member, axis=1))
    bias = jnp.concatenate(text_bias, axis=1)[:, :, None]

    attended, log_norm, highest = attend(queries, key_values, bias, sizes, head_dim)
    attn_out, _ = reduce_rows(*project(attended, o_near, o_far, sizes))
    mid, second_n, second_f = call(
        functools.partial(middle_kernel, sizes),
        [((per, width), F32), *halves],
        inputs,
        attn_out,
        modulation,
    )
    second = gather_rows(second_n, second_f)
    up_far = trade(after(up_near, second_n), "c")
    down_far = trade(after(down_near, second), "c")
    hidden, pre_grad = mlp(second, cot_rows, (up_near, up_far), (down_near, down_far), sizes)

    down_far_grad = stream_grads(cot_rows[1], hidden, sizes, False)
    up_far_grad = stream_grads(second[1], after(pre_grad, down_far_grad), sizes, False)
    hidden = after(hidden, up_far_grad)
    down_total = stream_grads(cot_rows[0], hidden, sizes, False, trade(down_far_grad, "c"))
    up_total = stream_grads(second[0], pre_grad, sizes, False, trade(up_far_grad, "c"))
    pre_grad = after(pre_grad, (down_total, up_total))
    second_grad, _ = reduce_rows(*project(pre_grad, up_near, up_far, sizes))
    down_shard, up_shard = shard_grad(down_total), shard_grad(up_total)
    mid_grad, attn_n, attn_f, two_sums = call(
        functools.partial(middle_back_kernel, sizes),
        [((per, width), F32), *halves, ((6 * seqs, width), F32)],
        mid,
        cot,
        second_grad,
        attn_out,
        modulation,
    )
    attn_rows = gather_rows(attn_n, attn_f)
    (mixed_grad,) = call(
        functools.partial(mixed_kernel, sizes),
        [(attended.shape, BF16)],
        *attn_rows,
        o_near,
        o_far,
    )
    mixed_grad = after(mixed_grad, (down_total, up_total))
    query_sum, kv_grads = attend_back(
        queries, key_values, bias, log_norm, mixed_grad, sizes, head_dim
    )
    h_low = (kv_grads[2].astype(F32) + trade(kv_grads[3], "c").astype(F32)).astype(BF16)
    h_grads = trade(h_low, "h")
    c_grads = trade(kv_grads[1], "c")

    mlp_out, _ = reduce_rows(*project(after(hidden, h_low), down_near, down_far, sizes))
    results, gate_sums = call(
        functools.partial(last_kernel, sizes),
        [((per, width), BF16), ((2 * seqs, width), F32)],
        mid,
        mlp_out,
        cot,
        modulation,
    )
    o_total = pair_grad(attn_rows, after(attended, query_sum), sizes)
    grad_down, grad_up = own_grad(down_shard), own_grad(up_shard)
    o_shard = shard_grad(after(o_total, up_shard))
    grad_o = own_grad(o_shard)

    low_all, gain_sums = call(
        functools.partial(qkv_back_kernel, sizes, head_dim),
        [((4 * per, 3 * heads * head_dim), BF16), (gains.shape, F32)],
        after(query_sum, (mlp_out, o_total)),
        kv_grads[0],
        c_grads,
        h_grads,
        raw,
        gains,
    )
    gain_terms = jnp.sum(gain_sums.reshape(2, 2, heads, head_dim), axis=2) * scales[None, :, None]
    low_all = after(low_all, (grad_down, grad_up, mlp_out, o_shard))
    grad_qkv = own_grad(shard_grad(pair_grad(first, low_all, sizes, True)))
    first_grad, _ = reduce_rows(*project(low_all, qkv_near, qkv_far, sizes))
    input_grads, one_sums = call(
        functools.partial(first_back_kernel, sizes),
        [((per, width), F32), ((4 * seqs, width), F32)],
        inputs,
        mid_grad,
        first_grad,
        modulation,
    )

    back = ((1,), (1,))

    def restore(moved):
        return (
            moved[:count_i].reshape(seqs, img_rows, width),
            moved[count_i:].reshape(seqs, txt_rows, width)[:, :txt_real],
        )

    out_img, out_txt = restore(
        lax.dot_general(results, order, (back, ((), ())), preferred_element_type=BF16)
    )
    grad_img, grad_txt = restore(permute_exact(input_grads, order, back))

    lanes = highest.shape[2] // 2
    row = jnp.arange(lanes, dtype=jnp.int32)
    valid = (row < 4 * img_rows) | ((row - 4 * img_rows) % txt_rows < txt_real)
    tops = highest.reshape(-1, seqs, 2, lanes)
    tops = jnp.max(jnp.where(valid, tops, -jnp.inf), axis=(1, 3)).reshape(1, heads)
    places = jnp.arange(4 * heads)[None, :] // heads
    tops = jnp.where(places == own["y"] * 2 + own["l"], jnp.tile(tops, (1, 4)), MASKED)

    count = 2 * seqs
    mod_low = jnp.concatenate(
        [one_sums, two_sums[2 * count :], two_sums[: 2 * count], gate_sums], axis=0
    ).astype(BF16)
    mod_count = mod_low.shape[0]
    mod_low = lax.dot_general(mod_low, order, (back, ((), ())), preferred_element_type=F32)
    extra = [gain_terms.reshape(1, -1), tops]
    extra = jnp.concatenate([jnp.pad(e, ((0, 0), (0, feat - e.shape[1]))) for e in extra])
    extra = jnp.pad(extra, ((0, -(mod_count + 2) % 8), (0, 0)))
    mod_low = jnp.concatenate([mod_low, jnp.tile(extra, (1, width // feat))], axis=0)
    is_top = jnp.arange(mod_low.shape[0])[:, None] == mod_count + 1

    def join(first, second):
        return jnp.where(is_top, jnp.maximum(first, second), first + second)

    quarters = [mod_low[:, k * feat : (k + 1) * feat] for k in range(width // feat)]
    at_c, at_y = own["c"] == 0, own["y"] == 0
    keep = [jnp.where(at_c, quarters[2 * k], quarters[2 * k + 1]) for k in range(2)]
    send = [jnp.where(at_c, quarters[2 * k + 1], quarters[2 * k]) for k in range(2)]
    pair = join(jnp.stack(keep), trade(jnp.stack(send), "c"))
    mod_sum = join(
        jnp.where(at_y, pair[0], pair[1]), trade(jnp.where(at_y, pair[1], pair[0]), "y")
    )
    for axis in ("l", "h"):
        mod_sum = join(mod_sum, trade(mod_sum, axis))
    if shard_count == 2:
        mod_members = jnp.stack([mod_sum, trade(mod_sum, "s")])
    else:
        mod_members = lax.all_gather(mod_sum, "s")
    gain_grad = jnp.sum(mod_members[:, mod_count], axis=0)[: 4 * head_dim]
    gain_grad = gain_grad.reshape(norm_gain.shape)
    tops = jnp.max(mod_members[:, mod_count + 1], axis=0)[: 4 * heads]
    peaks = lax.dynamic_slice_in_dim(tops, (own["y"] * 2 + own["c"]) * heads, heads)
    mod_seqs = mod_members[:, :mod_count].astype(BF16).reshape(-1, 6, 2, seqs, feat)
    mod_seqs = mod_seqs.transpose(2, 0, 3, 1, 4).reshape(2, -1, 6, feat)
    grad_mod = jnp.einsum("sd,tskf->tdkf", cond_rows, mod_seqs, preferred_element_type=F32)
    cond_part = jnp.einsum("tskf,tdkf->sd", mod_seqs, mod_w, preferred_element_type=F32)
    cond_part = in_order(in_order(total_over(cond_part, ("c", "y")), "l", 1), "h", 1)
    if shard_count == 2:
        mine, other = cond_part[:seqs], trade(cond_part[seqs:], "s")
        at_s = own["s"] == 0
        cond_total = jnp.concatenate(
            [jnp.where(at_s, mine, other), jnp.where(at_s, other, mine)], axis=1
        )
    else:
        cond_cols = lax.all_gather(cond_part, "s", axis=1, tiled=True)
        cond_total = lax.dynamic_slice_in_dim(cond_cols, own["s"] * seqs, seqs, axis=0)
    unused, silu_vjp = jax.vjp(jax.nn.silu, cond_float)
    grad_cond = silu_vjp(cond_total)[0]

    factor = jnp.sqrt(threshold / jnp.maximum(peaks, threshold))
    columns = jnp.repeat(factor, head_dim)
    clipped = qkv_w[:, :2].astype(F32) * columns
    return (
        out_img,
        out_txt,
        grad_img,
        grad_txt,
        grad_cond,
        grad_mod,
        grad_qkv,
        jnp.swapaxes(grad_o, 1, 2),
        grad_up,
        jnp.swapaxes(grad_down, 1, 2),
        gain_grad,
        clipped,
        peaks,
    )


def solution(mesh):
    shard, ctx, tp = (mesh.shape[name] for name in ("shard", "ctx", "tp"))
    fine = Mesh(mesh.devices.reshape(shard, ctx // 2, 2, tp // 2, 2), ("s", "h", "l", "y", "c"))
    ctx_axes, tp_axes = ("h", "l"), ("y", "c")
    rows = P("s", ctx_axes + tp_axes, None)
    weight = ("s",) + ctx_axes
    mod = P(None, weight, None, tp_axes)
    qkv = P(None, None, weight, tp_axes)
    inward = P(None, tp_axes, weight)
    outward = P(None, weight, tp_axes)
    return jax.shard_map(
        local,
        mesh=fine,
        in_specs=(
            rows,
            rows,
            P("s", None),
            P("s"),
            mod,
            qkv,
            inward,
            outward,
            inward,
            P(),
            P(),
            rows,
            rows,
        ),
        out_specs=(
            rows,
            rows,
            rows,
            rows,
            P("s", None),
            mod,
            qkv,
            inward,
            outward,
            inward,
            P(),
            qkv,
            P(tp_axes),
        ),
        check_vma=False,
    )
```
